32 devices in a mesh: row: 8 (over z, core), col: 4 (over y, x).
Axes of the slice: x: 2, y: 2, z: 4, core: 2. Of those that a mesh axis runs over, the one named last changes fastest.
Arguments:
- shot_traces: float32 [16384, 2, 8192], P(('row', 'col')), may hold values from -0.046875 to 0.046875
- shot_ids: int32 [16384], P(('row', 'col')), may hold values from 0 to 8191, as said below
- shot_counts: int32 [32], P(('row', 'col')), may hold values from 0 to 512, as said below
- missing_blocks: int32 [64, 64], P('row', 'col'), may hold values from 0 to 1, as said below
- weight_bins: int32 [8192], P(('row', 'col')), may hold values from 0 to 63
- weight_table: float32 [64], replicated, may hold values from 0.1 to 1
- focus_panel: float32 [2, 8192, 512], P(None, ('col', 'row')), may hold values from -6 to 6
Outputs:
- wavefield: float32 [2, 8192, 512], P(None, ('row', 'col'))
- adjoint_image: float32 [2, 8192, 512], P(None, ('col', 'row'))
The draws below stay inside these ranges and needn't reach their ends.
Inputs may be any that keep to these rules, and one draw needn't show every extreme that they name: `shot_ids`: over the counted slots of all devices every source appears exactly once; uncounted slots hold arbitrary sources. The counted slots of one device hold at most 64 sources of any block of 1024 consecutive sources, and at most (128) of any block of 2048; some device reaches both. `shot_counts`: some device has all 512 slots counted. `missing_blocks`: diagonal blocks are recorded, and of two mirrored blocks at most one is missing.
All inputs are finite; a program needn't handle non-finite values.
Results may differ from the reference program's by a relative error of at most 0.00007.
Values sent between devices are 32-bit elements; how exact they have to be, the bound alone decides.
A program may use at most 320 MiB of HBM per device.

```python
import math
import jax
import jax.numpy as jnp
from jax import lax

STATIONS = 8192
FOCUS = 512
BLOCK = 128
NBIN = 64
SRC_TILE = 1024
CAP = 64
SLOTS = 512
NBLK = 64
N_ROW = 8
DEVICES = 32


def assign_shots(key):
    base_key = jax.random.fold_in(key, 7)
    keys = jax.random.split(base_key, 5)
    pairing = jax.random.permutation(keys[0], DEVICES).astype(jnp.int32)
    share_first = jax.random.randint(keys[1], (DEVICES // 2, N_ROW), 0, CAP + 1).astype(jnp.int32)
    share_first = share_first.at[0].set(CAP)
    per_block = jnp.zeros((DEVICES, N_ROW), jnp.int32)
    per_block = per_block.at[pairing[0::2]].set(share_first)
    per_block = per_block.at[pairing[1::2]].set(CAP - share_first)
    offsets = jnp.cumsum(per_block, axis=0) - per_block
    orders = jax.vmap(lambda item: jax.random.permutation(item, SRC_TILE))(jax.random.split(keys[2], N_ROW)).astype(jnp.int32)
    within = jnp.arange(CAP, dtype=jnp.int32)
    has_shot = within[None, None, :] < per_block[:, :, None]
    in_block = jnp.where(has_shot, offsets[:, :, None] + within[None, None, :], 0)
    block_rows = jnp.arange(N_ROW, dtype=jnp.int32)[None, :, None]
    sources = block_rows * SRC_TILE + orders[block_rows, in_block]
    slot_start = jnp.cumsum(per_block, axis=1) - per_block
    slot_place = slot_start[:, :, None] + within[None, None, :]
    totals = jnp.sum(per_block, axis=1).astype(jnp.int32)
    scores = jax.random.randint(keys[3], (DEVICES, SLOTS), 0, 1 << 20).astype(jnp.int32) * SLOTS + jnp.arange(SLOTS, dtype=jnp.int32)[None, :]
    is_used = jnp.arange(SLOTS, dtype=jnp.int32)[None, :] < totals[:, None]
    scores = jnp.where(is_used, scores, jnp.int32(2147000000))
    ordering = jnp.argsort(scores, axis=1, stable=True)
    new_place = jnp.argsort(ordering, axis=1, stable=True).astype(jnp.int32)
    device_rows = jnp.broadcast_to(jnp.arange(DEVICES, dtype=jnp.int32)[:, None, None], sources.shape)
    moved = new_place[device_rows, jnp.where(has_shot, slot_place, 0)]
    moved = jnp.where(has_shot, moved, SLOTS)
    filler = jax.random.randint(keys[4], (DEVICES, SLOTS), 0, STATIONS).astype(jnp.int32)
    labels = filler.at[device_rows, moved].set(sources, mode='drop')
    return (labels.reshape(-1), totals)


def draw_shot_ids(key, part):
    return assign_shots(key)[0]


def draw_shot_counts(key, part):
    return assign_shots(key)[1]


def draw_missing_blocks(key, part):
    picks = jax.random.randint(jax.random.fold_in(key, 11), (NBLK, NBLK), 0, 10)
    indices = jnp.arange(NBLK, dtype=jnp.int32)
    above = indices[:, None] < indices[None, :]
    upper_missing = (picks < 2) & above
    lower_missing = (picks >= 2) & (picks < 4) & above
    return (upper_missing | lower_missing.T).astype(jnp.int32)


def place_ends(entries, key, smallest, top_value):
    extent = entries.shape
    index_at = [jax.random.randint(jax.random.fold_in(key, axis), (), 0, extent[axis]) for axis in range(len(extent))]
    entries = entries.at[tuple(index_at)].set(smallest)
    longest = extent.index(max(extent))
    index_at[longest] = (index_at[longest] + 1) % extent[longest]
    return entries.at[tuple(index_at)].set(top_value)


def shard_levels(key, extent, pieces, low, top_value):
    gain, own = 1.0, jax.random.fold_in(key, 6)
    for axis_at, blocks in pieces:
        draws = jnp.exp(jax.random.uniform(jax.random.fold_in(own, axis_at), (blocks,), jnp.float32, low / len(pieces), top_value / len(pieces)))
        gain = gain * jnp.repeat(draws, extent[axis_at] // blocks).reshape([-1 if axis == axis_at else 1 for axis in range(len(extent))])
    return gain


def noise(key, dims, scale, limit, pieces=(), kind=jnp.bfloat16):
    loudness = shard_levels(key, dims, pieces, -0.22, 0.18) if pieces else 1.0
    result = jax.random.normal(key, dims, jnp.float32) * scale * loudness
    return jnp.minimum(jnp.maximum(result, -limit), limit).astype(kind)


def setup_inputs(seed: int = 0) -> dict:
    streams_of = jax.random.split(jax.random.key(seed), 8)
    return {
        "shot_traces": noise(streams_of[0], (DEVICES * SLOTS, 2, STATIONS), (2 * STATIONS) ** -0.5, 0.046875, ((0, 32),), jnp.float32),
        "shot_ids": draw_shot_ids(jax.random.fold_in(streams_of[7], 71), 0),
        "shot_counts": draw_shot_counts(jax.random.fold_in(streams_of[7], 71), 0),
        "missing_blocks": draw_missing_blocks(jax.random.fold_in(streams_of[7], 71), 0),
        "weight_bins": place_ends(jax.random.randint(streams_of[4], (STATIONS,), 0, NBIN), jax.random.fold_in(streams_of[4], 1), 0, NBIN - 1).astype(jnp.int32),
        "weight_table": jnp.clip(jnp.exp(jax.random.uniform(streams_of[5], (NBIN,), jnp.float32, math.log(0.1), math.log(1.0))), 0.1, 1.0),
        "focus_panel": noise(streams_of[6], (2, STATIONS, FOCUS), 1.0, 6.0, ((1, 32),), jnp.float32),
    }


def high_dot(left, right):
    return jnp.dot(left, right, precision=lax.Precision.HIGHEST, preferred_element_type=jnp.float32)


def reference(shot_traces, shot_ids, shot_counts, missing_blocks, weight_bins, weight_table, focus_panel):
    slot_total = shot_traces.shape[0]
    slot_index = jnp.arange(slot_total, dtype=jnp.int32)
    counted = (slot_index % SLOTS) < jnp.repeat(shot_counts, SLOTS)
    target = jnp.where(counted, shot_ids, STATIONS).astype(jnp.int32)
    owner_slot = jnp.zeros((STATIONS,), jnp.int32).at[target].set(slot_index, mode="drop")
    kernel = shot_traces[owner_slot]
    missing_mask = jnp.repeat(jnp.repeat(missing_blocks > 0, BLOCK, axis=0), BLOCK, axis=1)
    kernel_re = jnp.where(missing_mask, kernel[:, 0, :].T, kernel[:, 0, :])
    kernel_im = jnp.where(missing_mask, kernel[:, 1, :].T, kernel[:, 1, :])
    panel_re = focus_panel[0]
    panel_im = focus_panel[1]
    field_re = high_dot(kernel_re, panel_re) - high_dot(kernel_im, panel_im)
    field_im = high_dot(kernel_re, panel_im) + high_dot(kernel_im, panel_re)
    weights = weight_table[weight_bins]
    weighted_re = weights[:, None] * field_re
    weighted_im = weights[:, None] * field_im
    image_re = high_dot(kernel_re.T, weighted_re) + high_dot(kernel_im.T, weighted_im)
    image_im = high_dot(kernel_re.T, weighted_im) - high_dot(kernel_im.T, weighted_re)
    return jnp.stack([field_re, field_im]), jnp.stack([image_re, image_im])
```

```python
import functools

import jax
import jax.numpy as jnp
from jax import lax
from jax.experimental import pallas as pl
from jax.experimental.pallas import tpu as pltpu
from jax.sharding import Mesh
from jax.sharding import PartitionSpec as P

AXES = ("z", "core", "col")
PIECES = 2
VMEM = 56 * 1024 * 1024
NT = (((1,), (1,)), ((), ()))
NN = (((1,), (0,)), ((), ()))


def params():
    return pltpu.CompilerParams(vmem_limit_bytes=VMEM)


def cost(flops, nbytes):
    return pl.CostEstimate(flops=int(flops), bytes_accessed=int(nbytes), transcendentals=0)


def mm(left, right, dims):
    return lax.dot_general(left, right, dims, preferred_element_type=jnp.float32)


def split(x):
    high = x.astype(jnp.bfloat16)
    return high, (x - high.astype(jnp.float32)).astype(jnp.bfloat16)


def pack_kernel(away_ref, keep_ref, away_in, keep_in, away_out, keep_out):
    for part in range(2):
        away_out[part] = away_in[:, part, :]
        keep_out[part] = keep_in[:, part, :]


def pack(traces, away, keep, width):
    slots, _, stations = traces.shape
    count = keep.shape[0]
    shape = jax.ShapeDtypeStruct((2, slots, count * width), jnp.float32)
    if width % 128:
        return tuple(
            jnp.concatenate(
                [
                    lax.dynamic_slice(traces, (0, 0, which[k] * width), (slots, 2, width))
                    for k in range(count)
                ],
                axis=2,
            ).transpose(1, 0, 2)
            for which in (away, keep)
        )
    out_spec = pl.BlockSpec((2, slots, width), lambda k, a, b: (0, 0, k))
    return pl.pallas_call(
        pack_kernel,
        grid_spec=pltpu.PrefetchScalarGridSpec(
            num_scalar_prefetch=2,
            grid=(count,),
            in_specs=[
                pl.BlockSpec((slots, 2, width), lambda k, a, b: (0, 0, a[k])),
                pl.BlockSpec((slots, 2, width), lambda k, a, b: (0, 0, b[k])),
            ],
            out_specs=[out_spec, out_spec],
        ),
        out_shape=[shape, shape],
        compiler_params=params(),
        cost_estimate=cost(0, 4 * traces.size * 4 // 2),
        name="pack",
    )(away, keep, traces, traces)


def prepare_kernel(
    keep_ref, got_ref, ids_ref, hot_ref, recorded_ref, mirrored_ref, target_ref,
    own_ref, mir_ref, place_ref
):
    slots = keep_ref.shape[1]
    for h, traces in enumerate((keep_ref, got_ref)):
        at = pl.ds(h * slots, slots)
        hot = hot_ref[at, :]
        own = mm(hot, recorded_ref[...], NN) > 0.5
        mir = mm(hot, mirrored_ref[...], NN) > 0.5
        place_ref[at, :] = jnp.where(ids_ref[at, :] == target_ref[...], 1.0, 0.0).astype(
            jnp.bfloat16
        )
        for part in range(2):
            high, low = split(traces[part])
            for t, piece in enumerate((high, low)):
                wide = piece.astype(jnp.float32)
                own_ref[2 * part + t, at, :] = jnp.where(own, wide, 0.0).astype(jnp.bfloat16)
                mir_ref[2 * part + t, at, :] = jnp.where(mir, wide, 0.0).astype(jnp.bfloat16)


def prepare(keep, got, ids, hot, recorded, mirrored, target):
    _, slots, length = keep.shape
    blocks = hot.shape[1]
    tile = min(256, length)
    traces_spec = pl.BlockSpec((2, slots, tile), lambda k: (0, 0, k))
    whole = lambda shape: pl.BlockSpec(shape, lambda k: (0, 0))
    strip = lambda rows: pl.BlockSpec((rows, tile), lambda k: (0, k))
    out_spec = pl.BlockSpec((4, 2 * slots, tile), lambda k: (0, 0, k))
    big = jax.ShapeDtypeStruct((4, 2 * slots, length), jnp.bfloat16)
    return pl.pallas_call(
        prepare_kernel,
        grid=(length // tile,),
        in_specs=[
            traces_spec,
            traces_spec,
            whole((2 * slots, 1)),
            whole((2 * slots, blocks)),
            strip(blocks),
            strip(blocks),
            strip(1),
        ],
        out_specs=[out_spec, out_spec, strip(2 * slots)],
        out_shape=[big, big, jax.ShapeDtypeStruct((2 * slots, length), jnp.bfloat16)],
        compiler_params=params(),
        cost_estimate=cost(0, 60 * slots * length),
        name="prepare",
    )(keep, got, ids, hot, recorded, mirrored, target)


def turn(real, imag, sign):
    return jnp.concatenate([imag * (-sign), real * sign], axis=0)


def to_slots_kernel(sign, re_ref, im_ref, k_ref, place_ref, o_ref):
    real, imag = re_ref[...], im_ref[...]
    high, low = split(jnp.concatenate([real, imag], axis=0))
    high2, low2 = split(turn(real, imag, sign))
    place = place_ref[...]
    made = (
        mm(high, k_ref[0], NT)
        + mm(low, k_ref[0], NT)
        + mm(high, k_ref[1], NT)
        + mm(high2, k_ref[2], NT)
        + mm(low2, k_ref[2], NT)
        + mm(high2, k_ref[3], NT)
    )
    picked = mm(high, place, NT) + mm(low, place, NT)

    @pl.when(pl.program_id(0) == 0)
    def _():
        o_ref[0] = made
        o_ref[1] = picked

    @pl.when(pl.program_id(0) > 0)
    def _():
        o_ref[0] += made
        o_ref[1] += picked


def to_slots(real, imag, kernel, place, sign):
    cols, length = real.shape
    slots = place.shape[0]
    tile = min(512, length)
    vec = pl.BlockSpec((cols, tile), lambda k: (0, k))
    return pl.pallas_call(
        functools.partial(to_slots_kernel, sign),
        grid=(length // tile,),
        in_specs=[
            vec,
            vec,
            pl.BlockSpec((4, slots, tile), lambda k: (0, 0, k)),
            pl.BlockSpec((slots, tile), lambda k: (0, k)),
        ],
        out_specs=pl.BlockSpec((2, 2 * cols, slots), lambda k: (0, 0, 0)),
        out_shape=jax.ShapeDtypeStruct((2, 2 * cols, slots), jnp.float32),
        compiler_params=params(),
        cost_estimate=cost(32 * cols * slots * length, 10 * slots * length),
        name="to_slots",
    )(real, imag, kernel, place)


def from_slots_kernel(
    sign, mine_ref, other_ref, k_ref, place_ref, re_ref, im_ref, made, picked
):
    cols = re_ref.shape[0]
    slots = place_ref.shape[0]
    half = slots // 2

    @pl.when(pl.program_id(0) == 0)
    def _():
        def total(t):
            return mine_ref[t] + jnp.concatenate(
                [other_ref[t, :, half:], other_ref[t, :, :half]], axis=1
            )

        made[0], made[1] = split(total(0))
        vec = total(1)
        picked[0], picked[1] = split(vec)
        picked[2], picked[3] = split(turn(vec[:cols], vec[cols:], sign))

    place = place_ref[...]
    out = (
        mm(picked[0], k_ref[0], NN)
        + mm(picked[1], k_ref[0], NN)
        + mm(picked[0], k_ref[1], NN)
        + mm(picked[2], k_ref[2], NN)
        + mm(picked[3], k_ref[2], NN)
        + mm(picked[2], k_ref[3], NN)
        + mm(made[0], place, NN)
        + mm(made[1], place, NN)
    )
    re_ref[...] = out[:cols]
    im_ref[...] = out[cols:]


def from_slots(mine, other, kernel, place, sign):
    slots, length = place.shape
    cols = mine.shape[1] // 2
    tile = min(512, length)
    whole = pl.BlockSpec((2, 2 * cols, slots), lambda k: (0, 0, 0))
    vec = pl.BlockSpec((cols, tile), lambda k: (0, k))
    shape = jax.ShapeDtypeStruct((cols, length), jnp.float32)
    return pl.pallas_call(
        functools.partial(from_slots_kernel, sign),
        grid=(length // tile,),
        in_specs=[
            whole,
            whole,
            pl.BlockSpec((4, slots, tile), lambda k: (0, 0, k)),
            pl.BlockSpec((slots, tile), lambda k: (0, k)),
        ],
        out_specs=[vec, vec],
        out_shape=[shape, shape],
        scratch_shapes=[
            pltpu.VMEM((2, 2 * cols, slots), jnp.bfloat16),
            pltpu.VMEM((4, 2 * cols, slots), jnp.bfloat16),
        ],
        compiler_params=params(),
        cost_estimate=cost(32 * cols * slots * length, 10 * slots * length),
        name="from_slots",
    )(mine, other, kernel, place)


def lookup(bins, table):
    matches = bins[:, None] == jnp.arange(table.shape[0], dtype=jnp.int32)[None, :]
    return jnp.sum(jnp.where(matches, table[None, :], 0.0), axis=1)


def local(
    zs, cols, shot_traces, shot_ids, shot_counts, missing_blocks, weight_bins, weight_table,
    focus_panel
):
    slots, _, stations = shot_traces.shape
    focus = focus_panel.shape[2]
    width = focus_panel.shape[1]
    rows = 2 * zs
    z, core, j = (lax.axis_index(name) for name in AXES)
    bits = [1 << b for b in range(cols.bit_length() - 1)]
    assert 1 << len(bits) == cols

    def device(a, c, b):
        return (a * 2 + c) * cols + b

    everyone = [(a, c, b) for a in range(zs) for c in range(2) for b in range(cols)]

    def send(x, target):
        return lax.ppermute(x, AXES, [(device(*d), device(*target(*d))) for d in everyone])

    def across_core(x):
        return send(x, lambda a, c, b: (a, 1 - c, b))

    def gather(piece, order):
        group = [piece] + [
            send(piece, lambda a, c, b, d=d: ((a - d) % zs, c, b)) for d in range(1, zs)
        ]
        size = zs * width
        groups = {0: jnp.concatenate(group, axis=1)}
        for bit in order:
            keys = sorted(groups)
            got = send(
                jnp.concatenate([groups[k] for k in keys], axis=1),
                lambda a, c, b: (a, c, b ^ bit),
            )
            for n, k in enumerate(keys):
                groups[k | bit] = got[:, n * size : (n + 1) * size]
        return jnp.concatenate([groups[k] for k in range(cols)], axis=1)

    def scatter(total, order):
        size = zs * width
        groups = {k: total[:, k * size : (k + 1) * size] for k in range(cols)}
        for bit in order:
            away = sorted(k for k in groups if k & bit)
            got = send(
                jnp.concatenate([groups[k] for k in away], axis=1),
                lambda a, c, b: (a, c, b ^ bit),
            )
            for n, k in enumerate(away):
                groups[k ^ bit] = groups[k ^ bit] + got[:, n * size : (n + 1) * size]
                del groups[k]
        line = groups[0]
        out = line[:, :width]
        for d in range(1, zs):
            out = out + send(
                line[:, d * width : (d + 1) * width],
                lambda a, c, b: ((a + d) % zs, c, b),
            )
        return out

    order_re, order_im = bits, bits[::-1]

    rel = [(q, d) for q in range(cols) for d in range(zs)]
    places = jnp.stack(
        [lax.bitwise_xor(j, jnp.int32(q)) * rows + lax.rem(z + d, zs) * 2 for q, d in rel]
    ).astype(jnp.int32)
    keep_at, away_at = places + core, places + 1 - core
    away, keep = pack(shot_traces, away_at, keep_at, width)
    got = across_core(away)

    counted = jnp.where(jnp.arange(slots, dtype=jnp.int32) < shot_counts[0], shot_ids, -1)
    ids = jnp.concatenate([counted, across_core(counted)])[:, None]
    missing = lax.all_gather(missing_blocks, ("z", "core"), axis=0, tiled=True)
    missing = lax.all_gather(missing, "col", axis=1, tiled=True).astype(jnp.bfloat16)
    blocks = missing.shape[0]
    side = stations // blocks
    hot = jnp.where(ids // side == jnp.arange(blocks, dtype=jnp.int32)[None, :], 1.0, 0.0)
    hot = jnp.where(ids >= 0, hot, 0.0).astype(jnp.bfloat16)
    target = (keep_at[:, None] * width + jnp.arange(width, dtype=jnp.int32)[None, :]).reshape(1, -1)
    spread = jnp.where(
        target // side == jnp.arange(blocks, dtype=jnp.int32)[:, None], 1.0, 0.0
    ).astype(jnp.bfloat16)
    recorded = mm(1 - missing, spread, NN).astype(jnp.bfloat16)
    mirrored = mm(missing.T, spread, NN).astype(jnp.bfloat16)
    own, mir, place = prepare(keep, got, ids, hot, recorded, mirrored, target)

    pairs = []
    for n in range(rows * cols):
        i, b = n % rows, n // rows
        pairs.append((n, i * cols + b))
    bins = lax.ppermute(weight_bins, AXES, pairs)
    weights = lookup(bins, weight_table)[None, :]
    back = [(b, a) for a, b in pairs]

    def product(real, imag, first, second, sign):
        real, imag = gather(real, order_re), gather(imag, order_im)
        mine = to_slots(real, imag, first, place, sign)
        real, imag = from_slots(mine, across_core(mine), second, place, sign)
        return scatter(real, order_re), scatter(imag, order_im)

    panel = focus_panel.transpose(0, 2, 1)
    step = focus // PIECES
    fields, images = [], []
    for h in range(PIECES):
        at = slice(h * step, (h + 1) * step)
        real, imag = product(panel[0, at], panel[1, at], own, mir, 1)
        fields.append(jnp.stack([real, imag]))
        real, imag = product(real * weights, imag * weights, mir, own, -1)
        images.append(jnp.stack([real, imag]))
    field = lax.ppermute(jnp.concatenate(fields, axis=1), AXES, back)
    return field.transpose(0, 2, 1), jnp.concatenate(images, axis=1).transpose(0, 2, 1)


def solution(mesh):
    rows, cols = mesh.shape["row"], mesh.shape["col"]
    zs = rows // 2
    split_mesh = Mesh(mesh.devices.reshape(zs, 2, cols), AXES)
    rowwise = ("z", "core", "col")
    colwise = ("col", "z", "core")
    placed = (
        P(rowwise, None, None),
        P(rowwise),
        P(rowwise),
        P(("z", "core"), "col"),
        P(rowwise),
        P(),
        P(None, colwise, None),
    )
    return jax.shard_map(
        functools.partial(local, zs, cols),
        mesh=split_mesh,
        in_specs=placed,
        out_specs=(P(None, rowwise, None), P(None, colwise, None)),
        check_vma=False,
    )
```

```python
import functools

import jax
import jax.numpy as jnp
from jax import lax
from jax.experimental import pallas as pl
from jax.experimental.pallas import tpu as pltpu
from jax.sharding import Mesh
from jax.sharding import PartitionSpec as P

AXES = ("z", "core", "col")
PIECES = 2
VMEM = 56 * 1024 * 1024
MEGA_VMEM = 60 * 1024 * 1024
TURNS = 4
NT = (((1,), (1,)), ((), ()))
NN = (((1,), (0,)), ((), ()))


def params():
    return pltpu.CompilerParams(vmem_limit_bytes=VMEM)


def cost(flops, nbytes):
    return pl.CostEstimate(flops=int(flops), bytes_accessed=int(nbytes), transcendentals=0)


def mm(left, right, dims):
    return lax.dot_general(left, right, dims, preferred_element_type=jnp.float32)


def split(x):
    high = x.astype(jnp.bfloat16)
    return high, (x - high.astype(jnp.float32)).astype(jnp.bfloat16)


def pack_kernel(away_ref, keep_ref, away_in, keep_in, away_out, keep_out):
    for part in range(2):
        away_out[part] = away_in[:, part, :]
        keep_out[part] = keep_in[:, part, :]


def pack(traces, away, keep, width):
    slots, _, stations = traces.shape
    count = keep.shape[0]
    shape = jax.ShapeDtypeStruct((2, slots, count * width), jnp.float32)
    if width % 128:
        return tuple(
            jnp.concatenate(
                [
                    lax.dynamic_slice(traces, (0, 0, which[k] * width), (slots, 2, width))
                    for k in range(count)
                ],
                axis=2,
            ).transpose(1, 0, 2)
            for which in (away, keep)
        )
    out_spec = pl.BlockSpec((2, slots, width), lambda k, a, b: (0, 0, k))
    return pl.pallas_call(
        pack_kernel,
        grid_spec=pltpu.PrefetchScalarGridSpec(
            num_scalar_prefetch=2,
            grid=(count,),
            in_specs=[
                pl.BlockSpec((slots, 2, width), lambda k, a, b: (0, 0, a[k])),
                pl.BlockSpec((slots, 2, width), lambda k, a, b: (0, 0, b[k])),
            ],
            out_specs=[out_spec, out_spec],
        ),
        out_shape=[shape, shape],
        compiler_params=params(),
        cost_estimate=cost(0, 4 * traces.size * 4 // 2),
        name="pack",
    )(away, keep, traces, traces)


def prepare_kernel(
    keep_ref, got_ref, ids_ref, hot_ref, recorded_ref, mirrored_ref, target_ref, both_ref,
    place_ref
):
    slots = keep_ref.shape[1]
    for h, traces in enumerate((keep_ref, got_ref)):
        at = pl.ds(h * slots, slots)
        hot = hot_ref[at, :]
        own = mm(hot, recorded_ref[...], NN) > 0.5
        mir = mm(hot, mirrored_ref[...], NN) > 0.5
        place_ref[at, :] = jnp.where(ids_ref[at, :] == target_ref[...], 1.0, 0.0).astype(
            jnp.bfloat16
        )
        for part in range(2):
            high, low = split(traces[part])
            for t, piece in enumerate((high, low)):
                wide = piece.astype(jnp.float32)
                both_ref[0, 2 * part + t, at, :] = jnp.where(own, wide, 0.0).astype(jnp.bfloat16)
                both_ref[1, 2 * part + t, at, :] = jnp.where(mir, wide, 0.0).astype(jnp.bfloat16)


def prepare(keep, got, ids, hot, recorded, mirrored, target):
    _, slots, length = keep.shape
    blocks = hot.shape[1]
    tile = min(256, length)
    traces_spec = pl.BlockSpec((2, slots, tile), lambda k: (0, 0, k))
    whole = lambda shape: pl.BlockSpec(shape, lambda k: (0, 0))
    strip = lambda rows: pl.BlockSpec((rows, tile), lambda k: (0, k))
    out_spec = pl.BlockSpec((2, 4, 2 * slots, tile), lambda k: (0, 0, 0, k))
    big = jax.ShapeDtypeStruct((2, 4, 2 * slots, length), jnp.bfloat16)
    return pl.pallas_call(
        prepare_kernel,
        grid=(length // tile,),
        in_specs=[
            traces_spec,
            traces_spec,
            whole((2 * slots, 1)),
            whole((2 * slots, blocks)),
            strip(blocks),
            strip(blocks),
            strip(1),
        ],
        out_specs=[out_spec, strip(2 * slots)],
        out_shape=[big, jax.ShapeDtypeStruct((2 * slots, length), jnp.bfloat16)],
        compiler_params=params(),
        cost_estimate=cost(0, 60 * slots * length),
        name="prepare",
    )(keep, got, ids, hot, recorded, mirrored, target)


def turn(real, imag, sign):
    return jnp.concatenate([imag * (-sign), real * sign], axis=0)


def to_slots_kernel(sign, re_ref, im_ref, k_ref, place_ref, o_ref):
    real, imag = re_ref[...], im_ref[...]
    high, low = split(jnp.concatenate([real, imag], axis=0))
    high2, low2 = split(turn(real, imag, sign))
    place = place_ref[...]
    made = (
        mm(high, k_ref[0], NT)
        + mm(low, k_ref[0], NT)
        + mm(high, k_ref[1], NT)
        + mm(high2, k_ref[2], NT)
        + mm(low2, k_ref[2], NT)
        + mm(high2, k_ref[3], NT)
    )
    picked = mm(high, place, NT) + mm(low, place, NT)

    @pl.when(pl.program_id(0) == 0)
    def _():
        o_ref[0] = made
        o_ref[1] = picked

    @pl.when(pl.program_id(0) > 0)
    def _():
        o_ref[0] += made
        o_ref[1] += picked


def to_slots(real, imag, kernel, place, sign):
    cols, length = real.shape
    slots = place.shape[0]
    tile = min(512, length)
    vec = pl.BlockSpec((cols, tile), lambda k: (0, k))
    return pl.pallas_call(
        functools.partial(to_slots_kernel, sign),
        grid=(length // tile,),
        in_specs=[
            vec,
            vec,
            pl.BlockSpec((4, slots, tile), lambda k: (0, 0, k)),
            pl.BlockSpec((slots, tile), lambda k: (0, k)),
        ],
        out_specs=pl.BlockSpec((2, 2 * cols, slots), lambda k: (0, 0, 0)),
        out_shape=jax.ShapeDtypeStruct((2, 2 * cols, slots), jnp.float32),
        compiler_params=params(),
        cost_estimate=cost(32 * cols * slots * length, 10 * slots * length),
        name="to_slots",
    )(real, imag, kernel, place)


def from_slots_kernel(
    sign, mine_ref, other_ref, k_ref, place_ref, re_ref, im_ref, made, picked
):
    cols = re_ref.shape[0]
    slots = place_ref.shape[0]
    half = slots // 2

    @pl.when(pl.program_id(0) == 0)
    def _():
        def total(t):
            return mine_ref[t] + jnp.concatenate(
                [other_ref[t, :, half:], other_ref[t, :, :half]], axis=1
            )

        made[0], made[1] = split(total(0))
        vec = total(1)
        picked[0], picked[1] = split(vec)
        picked[2], picked[3] = split(turn(vec[:cols], vec[cols:], sign))

    place = place_ref[...]
    out = (
        mm(picked[0], k_ref[0], NN)
        + mm(picked[1], k_ref[0], NN)
        + mm(picked[0], k_ref[1], NN)
        + mm(picked[2], k_ref[2], NN)
        + mm(picked[3], k_ref[2], NN)
        + mm(picked[2], k_ref[3], NN)
        + mm(made[0], place, NN)
        + mm(made[1], place, NN)
    )
    re_ref[...] = out[:cols]
    im_ref[...] = out[cols:]


def from_slots(mine, other, kernel, place, sign):
    slots, length = place.shape
    cols = mine.shape[1] // 2
    tile = min(512, length)
    whole = pl.BlockSpec((2, 2 * cols, slots), lambda k: (0, 0, 0))
    vec = pl.BlockSpec((cols, tile), lambda k: (0, k))
    shape = jax.ShapeDtypeStruct((cols, length), jnp.float32)
    return pl.pallas_call(
        functools.partial(from_slots_kernel, sign),
        grid=(length // tile,),
        in_specs=[
            whole,
            whole,
            pl.BlockSpec((4, slots, tile), lambda k: (0, 0, k)),
            pl.BlockSpec((slots, tile), lambda k: (0, k)),
        ],
        out_specs=[vec, vec],
        out_shape=[shape, shape],
        scratch_shapes=[
            pltpu.VMEM((2, 2 * cols, slots), jnp.bfloat16),
            pltpu.VMEM((4, 2 * cols, slots), jnp.bfloat16),
        ],
        compiler_params=params(),
        cost_estimate=cost(32 * cols * slots * length, 10 * slots * length),
        name="from_slots",
    )(mine, other, kernel, place)


def mega_kernel(
    zs, pieces, focus_ref, weights_ref, k_hbm, place_hbm, field_ref, image_ref,
    x, v, r1, r2, r3, ug, ug_got, vecs, kbuf, pbuf,
    ag_send, ag_recv, rs_send, rs_recv, ug_sem, k_sem, ready
):
    z, core, j = (lax.axis_index(name) for name in AXES)
    cols = 4
    step_cols, width = x.shape[3], x.shape[4]
    slots = ug.shape[2]
    half = slots // 2
    tile = 2 * width
    tiles = cols * zs // 2
    near_x = (z, core, j + 1 - 2 * (j % 2))
    near_y = (z, core, (j + 2) % 4)
    other = (z, 1 - core, j)

    def along(d):
        return ((z + d) % zs, core, j)

    first_to, second_to = (near_x, near_y), (near_y, near_x)
    first_at, second_at = (1, 2), (2, 1)
    peers = [near_x, near_y, other] + [along(d) for d in range(1, zs)]

    def remote(src, dst, send, recv, to):
        return pltpu.make_async_remote_copy(
            src_ref=src, dst_ref=dst, send_sem=send, recv_sem=recv, device_id=to,
            device_id_type=pl.DeviceIdType.MESH,
        )

    def spread(h, kind, p, d):
        if kind == 0:
            src, dst, to = 0, d, ((z + zs - d) % zs, core, j)
        elif kind == 1:
            src, dst, to = d, first_at[p] * zs + d, first_to[p]
        elif kind == 2:
            src, dst, to = d, second_at[p] * zs + d, second_to[p]
        else:
            src, dst, to = first_at[p] * zs + d, 3 * zs + d, second_to[p]
        at = (kind * 2 + p) * zs + d
        return remote(
            x.at[h, p, src], x.at[h, p, dst], ag_send.at[h, at], ag_recv.at[h, at], to
        )

    def spread_line(h):
        for p in range(2):
            for d in range(1, zs):
                spread(h, 0, p, d).start()
        for p in range(2):
            spread(h, 1, p, 0).start()
            spread(h, 2, p, 0).start()

    def spread_more(h, d):
        for p in range(2):
            spread(h, 0, p, d).wait_recv()
            spread(h, 1, p, d).start()
            spread(h, 2, p, d).start()

    def spread_last(h, d):
        for p in range(2):
            spread(h, 1, p, d).wait_recv()
            spread(h, 3, p, d).start()

    def spread_end(h):
        for p in range(2):
            for d in range(zs):
                if d:
                    spread(h, 0, p, d).wait_send()
                spread(h, 1, p, d).wait_send()
                spread(h, 2, p, d).wait()
                spread(h, 3, p, d).wait()

    def sum1(par, p, e, d):
        src = (first_at[p] if e == 0 else 3) * zs + d
        at = (p * 2 + e) * zs + d
        return remote(
            v.at[par, p, src], r1.at[p, e, d], rs_send.at[at], rs_recv.at[at], first_to[p]
        )

    def sum2(par, p, d):
        at = (4 + p) * zs + d
        return remote(
            v.at[par, p, second_at[p] * zs + d], r2.at[p, d], rs_send.at[at], rs_recv.at[at],
            second_to[p],
        )

    def sum3(par, p, d):
        at = (6 + p) * zs + d
        return remote(
            v.at[par, p, d], r3.at[p, d], rs_send.at[at], rs_recv.at[at], along(d)
        )

    def sum_first(par):
        for d in range(zs):
            for p in range(2):
                for e in range(2):
                    sum1(par, p, e, d).start()

    def sum_second(par, d):
        for p in range(2):
            for e in range(2):
                sum1(par, p, e, d).wait_recv()
            at = second_at[p] * zs + d
            v[par, p, at] += r1[p, 1, d]
            sum2(par, p, d).start()
            v[par, p, d] += r1[p, 0, d]

    def sum_third(par, d):
        for p in range(2):
            sum2(par, p, d).wait_recv()
            v[par, p, d] += r2[p, d]

            @pl.when(d > 0)
            def _():
                sum3(par, p, d).start()

    def sum_end(par, h, phase):
        for p in range(2):
            out = v[par, p, 0]
            for d in range(1, zs):
                sum3(par, p, d).wait_recv()
                out = out + r3[p, d]

            @pl.when(phase == 0)
            def _():
                field_ref[h, p] = out
                x[h, p, 0] = out * weights_ref[...]

            @pl.when(phase == 1)
            def _():
                image_ref[h, p] = out

        for p in range(2):
            for d in range(zs):
                for e in range(2):
                    sum1(par, p, e, d).wait_send()
                sum2(par, p, d).wait_send()
                if d:
                    sum3(par, p, d).wait_send()

    def fetch(which, k, buf):
        at = pl.ds(pl.multiple_of(k * tile, tile), tile)
        return (
            pltpu.make_async_copy(k_hbm.at[which, :, :, at], kbuf.at[buf], k_sem.at[buf, 0]),
            pltpu.make_async_copy(place_hbm.at[:, at], pbuf.at[buf], k_sem.at[buf, 1]),
        )

    def fetch_start(which, k, buf):
        for copy in fetch(which, k, buf):
            copy.start()

    def fetch_wait(which, k, buf):
        for copy in fetch(which, k, buf):
            copy.wait()

    def slots_step(h, k, buf, sign):
        real = jnp.concatenate([x[h, 0, 2 * k], x[h, 0, 2 * k + 1]], axis=1)
        imag = jnp.concatenate([x[h, 1, 2 * k], x[h, 1, 2 * k + 1]], axis=1)
        high, low = split(jnp.concatenate([real, imag], axis=0))
        high2, low2 = split(jnp.concatenate([imag * (-sign), real * sign], axis=0))
        place = pbuf[buf]
        ug[0] += (
            mm(high, kbuf[buf, 0], NT)
            + mm(low, kbuf[buf, 0], NT)
            + mm(high, kbuf[buf, 1], NT)
            + mm(high2, kbuf[buf, 2], NT)
            + mm(low2, kbuf[buf, 2], NT)
            + mm(high2, kbuf[buf, 3], NT)
        )
        ug[1] += mm(high, place, NT) + mm(low, place, NT)

    def vecs_make(sign):
        def total(t):
            return ug[t] + jnp.concatenate([ug_got[t, :, half:], ug_got[t, :, :half]], axis=1)

        vecs[0], vecs[1] = split(total(0))
        vec = total(1)
        vecs[2], vecs[3] = split(vec)
        vecs[4], vecs[5] = split(
            jnp.concatenate([vec[step_cols:] * (-sign), vec[:step_cols] * sign], axis=0)
        )

    def sources_step(par, k, buf):
        place = pbuf[buf]
        out = (
            mm(vecs[2], kbuf[buf, 0], NN)
            + mm(vecs[3], kbuf[buf, 0], NN)
            + mm(vecs[2], kbuf[buf, 1], NN)
            + mm(vecs[4], kbuf[buf, 2], NN)
            + mm(vecs[5], kbuf[buf, 2], NN)
            + mm(vecs[4], kbuf[buf, 3], NN)
            + mm(vecs[0], place, NN)
            + mm(vecs[1], place, NN)
        )
        for p in range(2):
            for e in range(2):
                v[par, p, 2 * k + e] = out[
                    p * step_cols : (p + 1) * step_cols, e * width : (e + 1) * width
                ]

    barrier = pltpu.get_barrier_semaphore()
    for peer in peers:
        pl.semaphore_signal(
            barrier, inc=1, device_id=peer, device_id_type=pl.DeviceIdType.MESH
        )
    for h in range(pieces):
        for p in range(2):
            x[h, p, 0] = focus_ref[p, h * step_cols : (h + 1) * step_cols]
    pl.semaphore_wait(barrier, len(peers))

    def loop(low, high, body):
        def step(i, carry):
            body(i)
            return carry

        lax.fori_loop(low, high, step, 0)

    loop(0, pieces, spread_line)
    loop(0, pieces, lambda h: loop(1, zs, lambda d: spread_more(h, d)))
    loop(0, pieces, lambda h: loop(0, zs, lambda d: spread_last(h, d)))
    fetch_start(0, 0, 0)

    def turn_of(t):
        for n, peer in enumerate(peers):
            pl.semaphore_signal(
                ready.at[n], inc=1, device_id=peer, device_id_type=pl.DeviceIdType.MESH
            )
        for n in range(len(peers)):
            pl.semaphore_wait(ready.at[n], 1)
        h, phase, par = t % pieces, t // pieces, t % 2
        sign = (1 - 2 * phase).astype(jnp.float32)
        computes = t < 2 * pieces
        sums = t > 0
        spreads = jnp.logical_and(t > 1, t < pieces + 2)
        h_sum, phase_sum, par_sum = (t + pieces - 1) % pieces, (t - 1) // pieces, (t + 1) % 2
        h_spread = (t + pieces - 2) % pieces

        @pl.when(sums)
        def _():
            sum_first(par_sum)

        @pl.when(spreads)
        def _():
            spread_line(h_spread)

        @pl.when(computes)
        def _():
            spread_end(h)
            ug[...] = jnp.zeros_like(ug)

        def first_half(d):
            @pl.when(computes)
            def _():
                for e in range(2):
                    k = 2 * d + e
                    fetch_wait(phase, k, e)
                    if e == 0:
                        fetch_start(phase, k + 1, 1)
                    else:
                        more = k + 1 < tiles

                        @pl.when(more)
                        def _():
                            fetch_start(phase, k + 1, 0)

                        @pl.when(jnp.logical_not(more))
                        def _():
                            fetch_start(1 - phase, 0, 0)

                    slots_step(h, k, e, sign)

            @pl.when(sums)
            def _():
                sum_second(par_sum, d)

            @pl.when(jnp.logical_and(spreads, d > 0))
            def _():
                spread_more(h_spread, d)

        loop(0, zs, first_half)

        @pl.when(computes)
        def _():
            swap = remote(ug, ug_got, ug_sem.at[0], ug_sem.at[1], other)
            swap.start()
            swap.wait()
            vecs_make(sign)

        def second_half(d):
            @pl.when(computes)
            def _():
                for e in range(2):
                    k = 2 * d + e
                    fetch_wait(1 - phase, k, e)
                    if e == 0:
                        fetch_start(1 - phase, k + 1, 1)
                    else:

                        @pl.when(k + 1 < tiles)
                        def _():
                            fetch_start(1 - phase, k + 1, 0)

                        @pl.when(jnp.logical_and(k + 1 == tiles, t + 1 < 2 * pieces))
                        def _():
                            fetch_start((t + 1) // pieces, 0, 0)

                    sources_step(par, k, e)

            @pl.when(sums)
            def _():
                sum_third(par_sum, d)

            @pl.when(spreads)
            def _():
                spread_last(h_spread, d)

        loop(0, zs, second_half)

        @pl.when(sums)
        def _():
            sum_end(par_sum, h_sum, phase_sum)

    loop(0, 2 * pieces + 1, turn_of)


def mega(panel, weights, kernels, place, zs, pieces):
    _, focus, width = panel.shape
    slots = place.shape[0]
    step = focus // pieces
    blocks = 4 * zs
    shape = jax.ShapeDtypeStruct((pieces, 2, step, width), jnp.float32)
    vmem = pl.BlockSpec(memory_space=pltpu.VMEM)
    hbm = pl.BlockSpec(memory_space=pl.ANY)
    f32, b16 = jnp.float32, jnp.bfloat16
    dma = pltpu.SemaphoreType.DMA
    return pl.pallas_call(
        functools.partial(mega_kernel, zs, pieces),
        in_specs=[vmem, vmem, hbm, hbm],
        out_specs=[vmem, vmem],
        out_shape=[shape, shape],
        scratch_shapes=[
            pltpu.VMEM((pieces, 2, blocks, step, width), f32),
            pltpu.VMEM((2, 2, blocks, step, width), f32),
            pltpu.VMEM((2, 2, zs, step, width), f32),
            pltpu.VMEM((2, zs, step, width), f32),
            pltpu.VMEM((2, zs, step, width), f32),
            pltpu.VMEM((2, 2 * step, slots), f32),
            pltpu.VMEM((2, 2 * step, slots), f32),
            pltpu.VMEM((6, 2 * step, slots), b16),
            pltpu.VMEM((2, 4, slots, 2 * width), b16),
            pltpu.VMEM((2, slots, 2 * width), b16),
            dma((pieces, 8 * zs)),
            dma((pieces, 8 * zs)),
            dma((8 * zs,)),
            dma((8 * zs,)),
            dma((2,)),
            dma((2, 2)),
            pltpu.SemaphoreType.REGULAR((zs + 2,)),
        ],
        compiler_params=pltpu.CompilerParams(
            collective_id=0, has_side_effects=True, vmem_limit_bytes=MEGA_VMEM
        ),
        name="products",
    )(panel, weights, kernels, place)


def lookup(bins, table):
    matches = bins[:, None] == jnp.arange(table.shape[0], dtype=jnp.int32)[None, :]
    return jnp.sum(jnp.where(matches, table[None, :], 0.0), axis=1)


def local(
    zs, cols, shot_traces, shot_ids, shot_counts, missing_blocks, weight_bins, weight_table,
    focus_panel
):
    slots, _, stations = shot_traces.shape
    focus = focus_panel.shape[2]
    width = focus_panel.shape[1]
    rows = 2 * zs
    z, core, j = (lax.axis_index(name) for name in AXES)
    bits = [1 << b for b in range(cols.bit_length() - 1)]
    assert 1 << len(bits) == cols

    def device(a, c, b):
        return (a * 2 + c) * cols + b

    everyone = [(a, c, b) for a in range(zs) for c in range(2) for b in range(cols)]

    def send(x, target):
        return lax.ppermute(x, AXES, [(device(*d), device(*target(*d))) for d in everyone])

    def across_core(x):
        return send(x, lambda a, c, b: (a, 1 - c, b))

    def gather(piece, order):
        group = [piece] + [
            send(piece, lambda a, c, b, d=d: ((a - d) % zs, c, b)) for d in range(1, zs)
        ]
        size = zs * width
        groups = {0: jnp.concatenate(group, axis=1)}
        for bit in order:
            keys = sorted(groups)
            got = send(
                jnp.concatenate([groups[k] for k in keys], axis=1),
                lambda a, c, b: (a, c, b ^ bit),
            )
            for n, k in enumerate(keys):
                groups[k | bit] = got[:, n * size : (n + 1) * size]
        return jnp.concatenate([groups[k] for k in range(cols)], axis=1)

    def scatter(total, order):
        size = zs * width
        groups = {k: total[:, k * size : (k + 1) * size] for k in range(cols)}
        for bit in order:
            away = sorted(k for k in groups if k & bit)
            got = send(
                jnp.concatenate([groups[k] for k in away], axis=1),
                lambda a, c, b: (a, c, b ^ bit),
            )
            for n, k in enumerate(away):
                groups[k ^ bit] = groups[k ^ bit] + got[:, n * size : (n + 1) * size]
                del groups[k]
        line = groups[0]
        out = line[:, :width]
        for d in range(1, zs):
            out = out + send(
                line[:, d * width : (d + 1) * width],
                lambda a, c, b: ((a + d) % zs, c, b),
            )
        return out

    order_re, order_im = bits, bits[::-1]

    rel = [(q, d) for q in range(cols) for d in range(zs)]
    places = jnp.stack(
        [lax.bitwise_xor(j, jnp.int32(q)) * rows + lax.rem(z + d, zs) * 2 for q, d in rel]
    ).astype(jnp.int32)
    keep_at, away_at = places + core, places + 1 - core
    away, keep = pack(shot_traces, away_at, keep_at, width)
    got = across_core(away)

    counted = jnp.where(jnp.arange(slots, dtype=jnp.int32) < shot_counts[0], shot_ids, -1)
    ids = jnp.concatenate([counted, across_core(counted)])[:, None]
    missing = lax.all_gather(missing_blocks, ("z", "core"), axis=0, tiled=True)
    missing = lax.all_gather(missing, "col", axis=1, tiled=True).astype(jnp.bfloat16)
    blocks = missing.shape[0]
    side = stations // blocks
    hot = jnp.where(ids // side == jnp.arange(blocks, dtype=jnp.int32)[None, :], 1.0, 0.0)
    hot = jnp.where(ids >= 0, hot, 0.0).astype(jnp.bfloat16)
    target = (keep_at[:, None] * width + jnp.arange(width, dtype=jnp.int32)[None, :]).reshape(1, -1)
    spread = jnp.where(
        target // side == jnp.arange(blocks, dtype=jnp.int32)[:, None], 1.0, 0.0
    ).astype(jnp.bfloat16)
    recorded = mm(1 - missing, spread, NN).astype(jnp.bfloat16)
    mirrored = mm(missing.T, spread, NN).astype(jnp.bfloat16)
    kernels, place = prepare(keep, got, ids, hot, recorded, mirrored, target)
    own, mir = kernels[0], kernels[1]

    pairs = []
    for n in range(rows * cols):
        i, b = n % rows, n // rows
        pairs.append((n, i * cols + b))
    bins = lax.ppermute(weight_bins, AXES, pairs)
    weights = lookup(bins, weight_table)[None, :]
    back = [(b, a) for a, b in pairs]

    def product(real, imag, first, second, sign):
        real, imag = gather(real, order_re), gather(imag, order_im)
        mine = to_slots(real, imag, first, place, sign)
        real, imag = from_slots(mine, across_core(mine), second, place, sign)
        return scatter(real, order_re), scatter(imag, order_im)

    panel = focus_panel.transpose(0, 2, 1)
    if cols == 4 and width % 128 == 0:
        field, image = mega(panel, weights, kernels, place, zs, TURNS)
        field, image = (
            out.transpose(1, 3, 0, 2).reshape(2, width, focus) for out in (field, image)
        )
        return lax.ppermute(field, AXES, back), image
    step = focus // PIECES
    fields, images = [], []
    for h in range(PIECES):
        at = slice(h * step, (h + 1) * step)
        real, imag = product(panel[0, at], panel[1, at], own, mir, 1)
        fields.append(jnp.stack([real, imag]))
        real, imag = product(real * weights, imag * weights, mir, own, -1)
        images.append(jnp.stack([real, imag]))
    field = lax.ppermute(jnp.concatenate(fields, axis=1), AXES, back)
    return field.transpose(0, 2, 1), jnp.concatenate(images, axis=1).transpose(0, 2, 1)


def solution(mesh):
    rows, cols = mesh.shape["row"], mesh.shape["col"]
    zs = rows // 2
    split_mesh = Mesh(mesh.devices.reshape(zs, 2, cols), AXES)
    rowwise = ("z", "core", "col")
    colwise = ("col", "z", "core")
    placed = (
        P(rowwise, None, None),
        P(rowwise),
        P(rowwise),
        P(("z", "core"), "col"),
        P(rowwise),
        P(),
        P(None, colwise, None),
    )
    return jax.shard_map(
        functools.partial(local, zs, cols),
        mesh=split_mesh,
        in_specs=placed,
        out_specs=(P(None, rowwise, None), P(None, colwise, None)),
        check_vma=False,
    )
```

```python
import functools

import jax
import jax.numpy as jnp
from jax import lax
from jax.experimental import pallas as pl
from jax.experimental.pallas import tpu as pltpu
from jax.sharding import Mesh
from jax.sharding import PartitionSpec as P

AXES = ("z", "core", "col")
PIECES = 2
VMEM = 56 * 1024 * 1024
MEGA_VMEM = 60 * 1024 * 1024
TURNS = 4
NT = (((1,), (1,)), ((), ()))
NN = (((1,), (0,)), ((), ()))


def params():
    return pltpu.CompilerParams(vmem_limit_bytes=VMEM)


def cost(flops, nbytes):
    return pl.CostEstimate(flops=int(flops), bytes_accessed=int(nbytes), transcendentals=0)


def mm(left, right, dims):
    return lax.dot_general(left, right, dims, preferred_element_type=jnp.float32)


def split(x):
    high = x.astype(jnp.bfloat16)
    return high, (x - high.astype(jnp.float32)).astype(jnp.bfloat16)


def pack_kernel(away_ref, keep_ref, away_in, keep_in, away_out, keep_out):
    for part in range(2):
        away_out[part] = away_in[:, part, :]
        keep_out[part] = keep_in[:, part, :]


def pack(traces, away, keep, width):
    slots, _, stations = traces.shape
    count = keep.shape[0]
    shape = jax.ShapeDtypeStruct((2, slots, count * width), jnp.float32)
    if width % 128:
        return tuple(
            jnp.concatenate(
                [
                    lax.dynamic_slice(traces, (0, 0, which[k] * width), (slots, 2, width))
                    for k in range(count)
                ],
                axis=2,
            ).transpose(1, 0, 2)
            for which in (away, keep)
        )
    out_spec = pl.BlockSpec((2, slots, width), lambda k, a, b: (0, 0, k))
    return pl.pallas_call(
        pack_kernel,
        grid_spec=pltpu.PrefetchScalarGridSpec(
            num_scalar_prefetch=2,
            grid=(count,),
            in_specs=[
                pl.BlockSpec((slots, 2, width), lambda k, a, b: (0, 0, a[k])),
                pl.BlockSpec((slots, 2, width), lambda k, a, b: (0, 0, b[k])),
            ],
            out_specs=[out_spec, out_spec],
        ),
        out_shape=[shape, shape],
        compiler_params=params(),
        cost_estimate=cost(0, 4 * traces.size * 4 // 2),
        name="pack",
    )(away, keep, traces, traces)


def prepare_kernel(
    keep_ref, got_ref, ids_ref, hot_ref, recorded_ref, mirrored_ref, target_ref, both_ref,
    place_ref
):
    slots = keep_ref.shape[1]
    for h, traces in enumerate((keep_ref, got_ref)):
        at = pl.ds(h * slots, slots)
        hot = hot_ref[at, :]
        own = mm(hot, recorded_ref[...], NN) > 0.5
        mir = mm(hot, mirrored_ref[...], NN) > 0.5
        place_ref[at, :] = jnp.where(ids_ref[at, :] == target_ref[...], 1.0, 0.0).astype(
            jnp.bfloat16
        )
        for part in range(2):
            high, low = split(traces[part])
            for t, piece in enumerate((high, low)):
                wide = piece.astype(jnp.float32)
                both_ref[0, 2 * part + t, at, :] = jnp.where(own, wide, 0.0).astype(jnp.bfloat16)
                both_ref[1, 2 * part + t, at, :] = jnp.where(mir, wide, 0.0).astype(jnp.bfloat16)


def prepare(keep, got, ids, hot, recorded, mirrored, target):
    _, slots, length = keep.shape
    blocks = hot.shape[1]
    tile = min(256, length)
    traces_spec = pl.BlockSpec((2, slots, tile), lambda k: (0, 0, k))
    whole = lambda shape: pl.BlockSpec(shape, lambda k: (0, 0))
    strip = lambda rows: pl.BlockSpec((rows, tile), lambda k: (0, k))
    out_spec = pl.BlockSpec((2, 4, 2 * slots, tile), lambda k: (0, 0, 0, k))
    big = jax.ShapeDtypeStruct((2, 4, 2 * slots, length), jnp.bfloat16)
    return pl.pallas_call(
        prepare_kernel,
        grid=(length // tile,),
        in_specs=[
            traces_spec,
            traces_spec,
            whole((2 * slots, 1)),
            whole((2 * slots, blocks)),
            strip(blocks),
            strip(blocks),
            strip(1),
        ],
        out_specs=[out_spec, strip(2 * slots)],
        out_shape=[big, jax.ShapeDtypeStruct((2 * slots, length), jnp.bfloat16)],
        compiler_params=params(),
        cost_estimate=cost(0, 60 * slots * length),
        name="prepare",
    )(keep, got, ids, hot, recorded, mirrored, target)


def turn(real, imag, sign):
    return jnp.concatenate([imag * (-sign), real * sign], axis=0)


def to_slots_kernel(sign, re_ref, im_ref, k_ref, place_ref, o_ref):
    real, imag = re_ref[...], im_ref[...]
    high, low = split(jnp.concatenate([real, imag], axis=0))
    high2, low2 = split(turn(real, imag, sign))
    place = place_ref[...]
    made = (
        mm(high, k_ref[0], NT)
        + mm(low, k_ref[0], NT)
        + mm(high, k_ref[1], NT)
        + mm(high2, k_ref[2], NT)
        + mm(low2, k_ref[2], NT)
        + mm(high2, k_ref[3], NT)
    )
    picked = mm(high, place, NT) + mm(low, place, NT)

    @pl.when(pl.program_id(0) == 0)
    def _():
        o_ref[0] = made
        o_ref[1] = picked

    @pl.when(pl.program_id(0) > 0)
    def _():
        o_ref[0] += made
        o_ref[1] += picked


def to_slots(real, imag, kernel, place, sign):
    cols, length = real.shape
    slots = place.shape[0]
    tile = min(512, length)
    vec = pl.BlockSpec((cols, tile), lambda k: (0, k))
    return pl.pallas_call(
        functools.partial(to_slots_kernel, sign),
        grid=(length // tile,),
        in_specs=[
            vec,
            vec,
            pl.BlockSpec((4, slots, tile), lambda k: (0, 0, k)),
            pl.BlockSpec((slots, tile), lambda k: (0, k)),
        ],
        out_specs=pl.BlockSpec((2, 2 * cols, slots), lambda k: (0, 0, 0)),
        out_shape=jax.ShapeDtypeStruct((2, 2 * cols, slots), jnp.float32),
        compiler_params=params(),
        cost_estimate=cost(32 * cols * slots * length, 10 * slots * length),
        name="to_slots",
    )(real, imag, kernel, place)


def from_slots_kernel(
    sign, mine_ref, other_ref, k_ref, place_ref, re_ref, im_ref, made, picked
):
    cols = re_ref.shape[0]
    slots = place_ref.shape[0]
    half = slots // 2

    @pl.when(pl.program_id(0) == 0)
    def _():
        def total(t):
            return mine_ref[t] + jnp.concatenate(
                [other_ref[t, :, half:], other_ref[t, :, :half]], axis=1
            )

        made[0], made[1] = split(total(0))
        vec = total(1)
        picked[0], picked[1] = split(vec)
        picked[2], picked[3] = split(turn(vec[:cols], vec[cols:], sign))

    place = place_ref[...]
    out = (
        mm(picked[0], k_ref[0], NN)
        + mm(picked[1], k_ref[0], NN)
        + mm(picked[0], k_ref[1], NN)
        + mm(picked[2], k_ref[2], NN)
        + mm(picked[3], k_ref[2], NN)
        + mm(picked[2], k_ref[3], NN)
        + mm(made[0], place, NN)
        + mm(made[1], place, NN)
    )
    re_ref[...] = out[:cols]
    im_ref[...] = out[cols:]


def from_slots(mine, other, kernel, place, sign):
    slots, length = place.shape
    cols = mine.shape[1] // 2
    tile = min(512, length)
    whole = pl.BlockSpec((2, 2 * cols, slots), lambda k: (0, 0, 0))
    vec = pl.BlockSpec((cols, tile), lambda k: (0, k))
    shape = jax.ShapeDtypeStruct((cols, length), jnp.float32)
    return pl.pallas_call(
        functools.partial(from_slots_kernel, sign),
        grid=(length // tile,),
        in_specs=[
            whole,
            whole,
            pl.BlockSpec((4, slots, tile), lambda k: (0, 0, k)),
            pl.BlockSpec((slots, tile), lambda k: (0, k)),
        ],
        out_specs=[vec, vec],
        out_shape=[shape, shape],
        scratch_shapes=[
            pltpu.VMEM((2, 2 * cols, slots), jnp.bfloat16),
            pltpu.VMEM((4, 2 * cols, slots), jnp.bfloat16),
        ],
        compiler_params=params(),
        cost_estimate=cost(32 * cols * slots * length, 10 * slots * length),
        name="from_slots",
    )(mine, other, kernel, place)


def mega_kernel(
    zs, pieces, panel_hbm, traces_hbm, weights_ref, ids_ref, hot_ref, recorded_ref,
    mirrored_ref, target_ref, field_ref, image_ref, k_hbm, place_hbm, got_hbm,
    x, v, r1, r2, r3, ug, ug_got, vecs, kbuf, pbuf, tbuf, stage,
    ag_send, ag_recv, rs_send, rs_recv, ug_sem, k_sem, ready,
    panel_sem, swap_send, swap_recv, in_sem, out_sem, field_send, field_recv
):
    z, core, j = (lax.axis_index(name) for name in AXES)
    cols = 4
    step_cols, width = x.shape[3], x.shape[4]
    slots = ug.shape[2]
    half = slots // 2
    tile = 2 * width
    tiles = cols * zs // 2
    near_x = (z, core, j + 1 - 2 * (j % 2))
    near_y = (z, core, (j + 2) % 4)
    other = (z, 1 - core, j)

    def along(d):
        return ((z + d) % zs, core, j)

    first_to, second_to = (near_x, near_y), (near_y, near_x)
    first_at, second_at = (1, 2), (2, 1)
    peers = [near_x, near_y, other] + [along(d) for d in range(1, zs)]
    rows = 2 * zs
    me = (z * 2 + core) * cols + j
    block = j * rows + z * 2 + core
    goal = (block // cols // 2, block // cols % 2, block % cols)
    origin = (me % rows // 2, me % rows % 2, me // rows)
    stays = block == me

    def remote(src, dst, send, recv, to):
        return pltpu.make_async_remote_copy(
            src_ref=src, dst_ref=dst, send_sem=send, recv_sem=recv, device_id=to,
            device_id_type=pl.DeviceIdType.MESH,
        )

    def spread(h, kind, p, d):
        if kind == 0:
            src, dst, to = 0, d, ((z + zs - d) % zs, core, j)
        elif kind == 1:
            src, dst, to = d, first_at[p] * zs + d, first_to[p]
        elif kind == 2:
            src, dst, to = d, second_at[p] * zs + d, second_to[p]
        else:
            src, dst, to = first_at[p] * zs + d, 3 * zs + d, second_to[p]
        at = (kind * 2 + p) * zs + d
        return remote(
            x.at[h, p, src], x.at[h, p, dst], ag_send.at[h, at], ag_recv.at[h, at], to
        )

    def spread_line(h):
        for p in range(2):
            for d in range(1, zs):
                spread(h, 0, p, d).start()
        for p in range(2):
            spread(h, 1, p, 0).start()
            spread(h, 2, p, 0).start()

    def spread_more(h, d):
        for p in range(2):
            spread(h, 0, p, d).wait_recv()
            spread(h, 1, p, d).start()
            spread(h, 2, p, d).start()

    def spread_last(h, d):
        for p in range(2):
            spread(h, 1, p, d).wait_recv()
            spread(h, 3, p, d).start()

    def spread_end(h):
        for p in range(2):
            for d in range(zs):
                if d:
                    spread(h, 0, p, d).wait_send()
                spread(h, 1, p, d).wait_send()
                spread(h, 2, p, d).wait()
                spread(h, 3, p, d).wait()

    def sum1(par, p, e, d):
        src = (first_at[p] if e == 0 else 3) * zs + d
        at = (p * 2 + e) * zs + d
        return remote(
            v.at[par, p, src], r1.at[p, e, d], rs_send.at[at], rs_recv.at[at], first_to[p]
        )

    def sum2(par, p, d):
        at = (4 + p) * zs + d
        return remote(
            v.at[par, p, second_at[p] * zs + d], r2.at[p, d], rs_send.at[at], rs_recv.at[at],
            second_to[p],
        )

    def sum3(par, p, d):
        at = (6 + p) * zs + d
        return remote(
            v.at[par, p, d], r3.at[p, d], rs_send.at[at], rs_recv.at[at], along(d)
        )

    def sum_first(par):
        for d in range(zs):
            for p in range(2):
                for e in range(2):
                    sum1(par, p, e, d).start()

    def sum_second(par, d):
        for p in range(2):
            for e in range(2):
                sum1(par, p, e, d).wait_recv()
            at = second_at[p] * zs + d
            v[par, p, at] += r1[p, 1, d]
            sum2(par, p, d).start()
            v[par, p, d] += r1[p, 0, d]

    def sum_third(par, d):
        for p in range(2):
            sum2(par, p, d).wait_recv()
            v[par, p, d] += r2[p, d]

            @pl.when(d > 0)
            def _():
                sum3(par, p, d).start()

    def deliver(h, action):
        @pl.when(stays)
        def _():
            getattr(
                pltpu.make_async_copy(stage.at[h], field_ref.at[h], field_send.at[h]), action
            )()

        @pl.when(jnp.logical_not(stays))
        def _():
            getattr(
                remote(
                    stage.at[h], field_ref.at[h], field_send.at[h], field_recv.at[h], goal
                ),
                action,
            )()

    def sum_end(par, h, phase):
        for p in range(2):
            out = v[par, p, 0]
            for d in range(1, zs):
                sum3(par, p, d).wait_recv()
                out = out + r3[p, d]

            @pl.when(phase == 0)
            def _():
                stage[h, p] = out
                x[h, p, 0] = out * weights_ref[...]

            @pl.when(phase == 1)
            def _():
                image_ref[h, p] = out

        @pl.when(phase == 0)
        def _():
            deliver(h, "start")

        for p in range(2):
            for d in range(zs):
                for e in range(2):
                    sum1(par, p, e, d).wait_send()
                sum2(par, p, d).wait_send()
                if d:
                    sum3(par, p, d).wait_send()

    def fetch(which, k, buf):
        at = pl.ds(pl.multiple_of(k * tile, tile), tile)
        return (
            pltpu.make_async_copy(k_hbm.at[which, :, :, at], kbuf.at[buf], k_sem.at[buf, 0]),
            pltpu.make_async_copy(place_hbm.at[:, at], pbuf.at[buf], k_sem.at[buf, 1]),
        )

    def fetch_start(which, k, buf):
        for copy in fetch(which, k, buf):
            copy.start()

    def fetch_wait(which, k, buf):
        for copy in fetch(which, k, buf):
            copy.wait()

    def slots_step(h, k, buf, sign):
        real = jnp.concatenate([x[h, 0, 2 * k], x[h, 0, 2 * k + 1]], axis=1)
        imag = jnp.concatenate([x[h, 1, 2 * k], x[h, 1, 2 * k + 1]], axis=1)
        high, low = split(jnp.concatenate([real, imag], axis=0))
        high2, low2 = split(jnp.concatenate([imag * (-sign), real * sign], axis=0))
        place = pbuf[buf]
        ug[0] += (
            mm(high, kbuf[buf, 0], NT)
            + mm(low, kbuf[buf, 0], NT)
            + mm(high, kbuf[buf, 1], NT)
            + mm(high2, kbuf[buf, 2], NT)
            + mm(low2, kbuf[buf, 2], NT)
            + mm(high2, kbuf[buf, 3], NT)
        )
        ug[1] += mm(high, place, NT) + mm(low, place, NT)

    def vecs_make(sign):
        def total(t):
            return ug[t] + jnp.concatenate([ug_got[t, :, half:], ug_got[t, :, :half]], axis=1)

        vecs[0], vecs[1] = split(total(0))
        vec = total(1)
        vecs[2], vecs[3] = split(vec)
        vecs[4], vecs[5] = split(
            jnp.concatenate([vec[step_cols:] * (-sign), vec[:step_cols] * sign], axis=0)
        )

    def sources_step(par, k, buf):
        place = pbuf[buf]
        out = (
            mm(vecs[2], kbuf[buf, 0], NN)
            + mm(vecs[3], kbuf[buf, 0], NN)
            + mm(vecs[2], kbuf[buf, 1], NN)
            + mm(vecs[4], kbuf[buf, 2], NN)
            + mm(vecs[5], kbuf[buf, 2], NN)
            + mm(vecs[4], kbuf[buf, 3], NN)
            + mm(vecs[0], place, NN)
            + mm(vecs[1], place, NN)
        )
        for p in range(2):
            for e in range(2):
                v[par, p, 2 * k + e] = out[
                    p * step_cols : (p + 1) * step_cols, e * width : (e + 1) * width
                ]

    def receivers(k):
        q, d = k // zs, k % zs
        col = (j + q) % 2 + 2 * ((j // 2 + q // 2) % 2)
        return col * rows + (z + d) % zs * 2

    def lanes(at):
        return pl.ds(pl.multiple_of(at * width, width), width)

    def swap(k):
        return remote(
            traces_hbm.at[:, :, lanes(receivers(k) + 1 - core)], got_hbm.at[k],
            swap_send.at[k], swap_recv.at[k], other,
        )

    def load(k, buf):
        return (
            pltpu.make_async_copy(
                traces_hbm.at[:, :, lanes(receivers(k) + core)], tbuf.at[buf, 0],
                in_sem.at[buf, 0],
            ),
            pltpu.make_async_copy(got_hbm.at[k], tbuf.at[buf, 1], in_sem.at[buf, 1]),
        )

    def load_start(k, buf):
        swap(k).wait_recv()
        for copy in load(k, buf):
            copy.start()

    def store(k, buf):
        return [
            pltpu.make_async_copy(
                kbuf.at[buf, :, :, pl.ds(which * width, width)],
                k_hbm.at[which, :, :, lanes(k)],
                out_sem.at[buf, which],
            )
            for which in range(2)
        ] + [
            pltpu.make_async_copy(
                pbuf.at[buf, :, pl.ds(0, width)], place_hbm.at[:, lanes(k)], out_sem.at[buf, 2]
            )
        ]

    def prepare_step(k, buf):
        part_slots = tbuf.shape[2]
        at = lanes(k)
        for half_at in range(2):
            these = pl.ds(half_at * part_slots, part_slots)
            hot = hot_ref[these, :]
            own = mm(hot, recorded_ref[:, at], NN) > 0.5
            mir = mm(hot, mirrored_ref[:, at], NN) > 0.5
            pbuf[buf, these, pl.ds(0, width)] = jnp.where(
                ids_ref[these, :] == target_ref[:, at], 1.0, 0.0
            ).astype(jnp.bfloat16)
            for part in range(2):
                high, low = split(tbuf[buf, half_at, :, part, :])
                for n, piece in enumerate((high, low)):
                    wide = piece.astype(jnp.float32)
                    for which, mask in enumerate((own, mir)):
                        kbuf[buf, 2 * part + n, these, pl.ds(which * width, width)] = jnp.where(
                            mask, wide, 0.0
                        ).astype(jnp.bfloat16)

    def loop(low, high, body):
        def step(i, carry):
            body(i)
            return carry

        lax.fori_loop(low, high, step, 0)

    barrier = pltpu.get_barrier_semaphore()
    for peer in peers:
        pl.semaphore_signal(
            barrier, inc=1, device_id=peer, device_id_type=pl.DeviceIdType.MESH
        )

    @pl.when(jnp.logical_not(stays))
    def _():
        for peer in (goal, origin):
            pl.semaphore_signal(
                barrier, inc=1, device_id=peer, device_id_type=pl.DeviceIdType.MESH
            )

    def own_piece(h, p):
        return pltpu.make_async_copy(
            panel_hbm.at[p, h], x.at[h, p, 0], panel_sem.at[h * 2 + p]
        )

    for h in range(pieces):
        for p in range(2):
            own_piece(h, p).start()
    for h in range(pieces):
        for p in range(2):
            own_piece(h, p).wait()

    @pl.when(stays)
    def _():
        pl.semaphore_wait(barrier, len(peers))

    @pl.when(jnp.logical_not(stays))
    def _():
        pl.semaphore_wait(barrier, len(peers) + 2)

    count = cols * zs
    loop(0, 2, spread_line)
    loop(0, count, lambda k: swap(k).start())
    load_start(0, 0)

    def prepare_pair(i):
        for e in range(2):
            k = 2 * i + e
            if e == 0:
                load_start(k + 1, 1)
            else:

                @pl.when(k + 1 < count)
                def _():
                    load_start(k + 1, 0)

            for copy in load(k, e):
                copy.wait()

            @pl.when(i > 0)
            def _():
                for copy in store(k - 2, e):
                    copy.wait()

            prepare_step(k, e)
            for copy in store(k, e):
                copy.start()
        h, d = i // zs, i % zs

        @pl.when(d > 0)
        def _():
            spread_more(h, d)

    loop(0, count // 2, prepare_pair)
    for e in range(2):
        for copy in store(count - 2 + e, e):
            copy.wait()
    loop(0, count, lambda k: swap(k).wait_send())
    fetch_start(0, 0, 0)
    loop(0, 2, lambda h: loop(0, zs, lambda d: spread_last(h, d)))

    def turn_of(t):
        for n, peer in enumerate(peers):
            pl.semaphore_signal(
                ready.at[n], inc=1, device_id=peer, device_id_type=pl.DeviceIdType.MESH
            )
        for n in range(len(peers)):
            pl.semaphore_wait(ready.at[n], 1)
        h, phase, par = t % pieces, t // pieces, t % 2
        sign = (1 - 2 * phase).astype(jnp.float32)
        computes = t < 2 * pieces
        sums = t > 0
        spreads = t < pieces + 2
        h_sum, phase_sum, par_sum = (t + pieces - 1) % pieces, (t - 1) // pieces, (t + 1) % 2
        h_spread = (t + pieces - 2) % pieces

        @pl.when(sums)
        def _():
            sum_first(par_sum)

        @pl.when(spreads)
        def _():
            spread_line(h_spread)

        @pl.when(computes)
        def _():
            spread_end(h)
            ug[...] = jnp.zeros_like(ug)

        def first_half(d):
            @pl.when(computes)
            def _():
                for e in range(2):
                    k = 2 * d + e
                    fetch_wait(phase, k, e)
                    if e == 0:
                        fetch_start(phase, k + 1, 1)
                    else:
                        more = k + 1 < tiles

                        @pl.when(more)
                        def _():
                            fetch_start(phase, k + 1, 0)

                        @pl.when(jnp.logical_not(more))
                        def _():
                            fetch_start(1 - phase, 0, 0)

                    slots_step(h, k, e, sign)

            @pl.when(sums)
            def _():
                sum_second(par_sum, d)

            @pl.when(jnp.logical_and(spreads, d > 0))
            def _():
                spread_more(h_spread, d)

        loop(0, zs, first_half)

        @pl.when(computes)
        def _():
            swap = remote(ug, ug_got, ug_sem.at[0], ug_sem.at[1], other)
            swap.start()
            swap.wait()
            vecs_make(sign)

        def second_half(d):
            @pl.when(computes)
            def _():
                for e in range(2):
                    k = 2 * d + e
                    fetch_wait(1 - phase, k, e)
                    if e == 0:
                        fetch_start(1 - phase, k + 1, 1)
                    else:

                        @pl.when(k + 1 < tiles)
                        def _():
                            fetch_start(1 - phase, k + 1, 0)

                        @pl.when(jnp.logical_and(k + 1 == tiles, t + 1 < 2 * pieces))
                        def _():
                            fetch_start((t + 1) // pieces, 0, 0)

                    sources_step(par, k, e)

            @pl.when(sums)
            def _():
                sum_third(par_sum, d)

            @pl.when(spreads)
            def _():
                spread_last(h_spread, d)

        loop(0, zs, second_half)

        @pl.when(sums)
        def _():
            sum_end(par_sum, h_sum, phase_sum)

    loop(0, 2 * pieces + 1, turn_of)
    loop(0, pieces, lambda h: deliver(h, "wait"))


def mega(panel, traces, weights, ids, hot, recorded, mirrored, target, zs, pieces):
    _, focus, width = panel.shape
    part_slots = traces.shape[0]
    slots = 2 * part_slots
    step = focus // pieces
    blocks = 4 * zs
    length = blocks * width
    panel = panel.reshape(2, pieces, step, width)
    vmem = pl.BlockSpec(memory_space=pltpu.VMEM)
    hbm = pl.BlockSpec(memory_space=pl.ANY)
    f32, b16 = jnp.float32, jnp.bfloat16
    dma = pltpu.SemaphoreType.DMA
    shape = jax.ShapeDtypeStruct((pieces, 2, step, width), f32)
    return pl.pallas_call(
        functools.partial(mega_kernel, zs, pieces),
        in_specs=[hbm, hbm] + [vmem] * 6,
        out_specs=[vmem, vmem, hbm, hbm, hbm],
        out_shape=[
            shape,
            shape,
            jax.ShapeDtypeStruct((2, 4, slots, length), b16),
            jax.ShapeDtypeStruct((slots, length), b16),
            jax.ShapeDtypeStruct((blocks, part_slots, 2, width), f32),
        ],
        scratch_shapes=[
            pltpu.VMEM((pieces, 2, blocks, step, width), f32),
            pltpu.VMEM((2, 2, blocks, step, width), f32),
            pltpu.VMEM((2, 2, zs, step, width), f32),
            pltpu.VMEM((2, zs, step, width), f32),
            pltpu.VMEM((2, zs, step, width), f32),
            pltpu.VMEM((2, 2 * step, slots), f32),
            pltpu.VMEM((2, 2 * step, slots), f32),
            pltpu.VMEM((6, 2 * step, slots), b16),
            pltpu.VMEM((2, 4, slots, 2 * width), b16),
            pltpu.VMEM((2, slots, 2 * width), b16),
            pltpu.VMEM((2, 2, part_slots, 2, width), f32),
            pltpu.VMEM((pieces, 2, step, width), f32),
            dma((pieces, 8 * zs)),
            dma((pieces, 8 * zs)),
            dma((8 * zs,)),
            dma((8 * zs,)),
            dma((2,)),
            dma((2, 2)),
            pltpu.SemaphoreType.REGULAR((zs + 2,)),
            dma((2 * pieces,)),
            dma((blocks,)),
            dma((blocks,)),
            dma((2, 2)),
            dma((2, 3)),
            dma((pieces,)),
            dma((pieces,)),
        ],
        compiler_params=pltpu.CompilerParams(
            collective_id=0, has_side_effects=True, vmem_limit_bytes=MEGA_VMEM
        ),
        name="products",
    )(panel, traces, weights, ids, hot, recorded, mirrored, target)[:2]


def lookup(bins, table):
    matches = bins[:, None] == jnp.arange(table.shape[0], dtype=jnp.int32)[None, :]
    return jnp.sum(jnp.where(matches, table[None, :], 0.0), axis=1)


def local(
    zs, cols, shot_traces, shot_ids, shot_counts, missing_blocks, weight_bins, weight_table,
    focus_panel
):
    slots, _, stations = shot_traces.shape
    focus = focus_panel.shape[2]
    width = focus_panel.shape[1]
    rows = 2 * zs
    z, core, j = (lax.axis_index(name) for name in AXES)
    bits = [1 << b for b in range(cols.bit_length() - 1)]
    assert 1 << len(bits) == cols

    def device(a, c, b):
        return (a * 2 + c) * cols + b

    everyone = [(a, c, b) for a in range(zs) for c in range(2) for b in range(cols)]

    def send(x, target):
        return lax.ppermute(x, AXES, [(device(*d), device(*target(*d))) for d in everyone])

    def across_core(x):
        return send(x, lambda a, c, b: (a, 1 - c, b))

    def gather(piece, order):
        group = [piece] + [
            send(piece, lambda a, c, b, d=d: ((a - d) % zs, c, b)) for d in range(1, zs)
        ]
        size = zs * width
        groups = {0: jnp.concatenate(group, axis=1)}
        for bit in order:
            keys = sorted(groups)
            got = send(
                jnp.concatenate([groups[k] for k in keys], axis=1),
                lambda a, c, b: (a, c, b ^ bit),
            )
            for n, k in enumerate(keys):
                groups[k | bit] = got[:, n * size : (n + 1) * size]
        return jnp.concatenate([groups[k] for k in range(cols)], axis=1)

    def scatter(total, order):
        size = zs * width
        groups = {k: total[:, k * size : (k + 1) * size] for k in range(cols)}
        for bit in order:
            away = sorted(k for k in groups if k & bit)
            got = send(
                jnp.concatenate([groups[k] for k in away], axis=1),
                lambda a, c, b: (a, c, b ^ bit),
            )
            for n, k in enumerate(away):
                groups[k ^ bit] = groups[k ^ bit] + got[:, n * size : (n + 1) * size]
                del groups[k]
        line = groups[0]
        out = line[:, :width]
        for d in range(1, zs):
            out = out + send(
                line[:, d * width : (d + 1) * width],
                lambda a, c, b: ((a + d) % zs, c, b),
            )
        return out

    order_re, order_im = bits, bits[::-1]

    rel = [(q, d) for q in range(cols) for d in range(zs)]
    places = jnp.stack(
        [lax.bitwise_xor(j, jnp.int32(q)) * rows + lax.rem(z + d, zs) * 2 for q, d in rel]
    ).astype(jnp.int32)
    keep_at, away_at = places + core, places + 1 - core
    counted = jnp.where(jnp.arange(slots, dtype=jnp.int32) < shot_counts[0], shot_ids, -1)
    ids = jnp.concatenate([counted, across_core(counted)])[:, None]
    down, over = missing_blocks.shape
    missing = lax.all_gather(missing_blocks, AXES).reshape(rows, cols, down, over)
    missing = missing.transpose(0, 2, 1, 3).reshape(rows * down, cols * over)
    missing = missing.astype(jnp.bfloat16)
    blocks = missing.shape[0]
    side = stations // blocks
    hot = jnp.where(ids // side == jnp.arange(blocks, dtype=jnp.int32)[None, :], 1.0, 0.0)
    hot = jnp.where(ids >= 0, hot, 0.0).astype(jnp.bfloat16)
    target = (keep_at[:, None] * width + jnp.arange(width, dtype=jnp.int32)[None, :]).reshape(1, -1)
    spread = jnp.where(
        target // side == jnp.arange(blocks, dtype=jnp.int32)[:, None], 1.0, 0.0
    ).astype(jnp.bfloat16)
    recorded = mm(1 - missing, spread, NN).astype(jnp.bfloat16)
    mirrored = mm(missing.T, spread, NN).astype(jnp.bfloat16)

    pairs = []
    for n in range(rows * cols):
        i, b = n % rows, n // rows
        pairs.append((n, i * cols + b))
    bins = lax.ppermute(weight_bins, AXES, pairs)
    weights = lookup(bins, weight_table)[None, :]
    back = [(b, a) for a, b in pairs]

    def product(real, imag, first, second, sign):
        real, imag = gather(real, order_re), gather(imag, order_im)
        mine = to_slots(real, imag, first, place, sign)
        real, imag = from_slots(mine, across_core(mine), second, place, sign)
        return scatter(real, order_re), scatter(imag, order_im)

    panel = focus_panel.transpose(0, 2, 1)
    if cols == 4 and width % 128 == 0:
        outs = mega(
            panel, shot_traces, weights, ids, hot, recorded, mirrored, target, zs, TURNS
        )
        return tuple(out.transpose(1, 3, 0, 2).reshape(2, width, focus) for out in outs)
    step = focus // PIECES
    away, keep = pack(shot_traces, away_at, keep_at, width)
    got = across_core(away)
    kernels, place = prepare(keep, got, ids, hot, recorded, mirrored, target)
    own, mir = kernels[0], kernels[1]
    fields, images = [], []
    for h in range(PIECES):
        at = slice(h * step, (h + 1) * step)
        real, imag = product(panel[0, at], panel[1, at], own, mir, 1)
        fields.append(jnp.stack([real, imag]))
        real, imag = product(real * weights, imag * weights, mir, own, -1)
        images.append(jnp.stack([real, imag]))
    field = lax.ppermute(jnp.concatenate(fields, axis=1), AXES, back)
    return field.transpose(0, 2, 1), jnp.concatenate(images, axis=1).transpose(0, 2, 1)


def solution(mesh):
    rows, cols = mesh.shape["row"], mesh.shape["col"]
    zs = rows // 2
    split_mesh = Mesh(mesh.devices.reshape(zs, 2, cols), AXES)
    rowwise = ("z", "core", "col")
    colwise = ("col", "z", "core")
    placed = (
        P(rowwise, None, None),
        P(rowwise),
        P(rowwise),
        P(("z", "core"), "col"),
        P(rowwise),
        P(),
        P(None, colwise, None),
    )
    return jax.shard_map(
        functools.partial(local, zs, cols),
        mesh=split_mesh,
        in_specs=placed,
        out_specs=(P(None, rowwise, None), P(None, colwise, None)),
        check_vma=False,
    )
```

```python
import functools

import jax
import jax.numpy as jnp
from jax import lax
from jax.experimental import pallas as pl
from jax.experimental.pallas import tpu as pltpu
from jax.sharding import Mesh
from jax.sharding import PartitionSpec as P

AXES = ("z", "core", "col")
PIECES = 2
VMEM = 56 * 1024 * 1024
MEGA_VMEM = 60 * 1024 * 1024
TURNS = 4
NT = (((1,), (1,)), ((), ()))
NN = (((1,), (0,)), ((), ()))


def params():
    return pltpu.CompilerParams(vmem_limit_bytes=VMEM)


def cost(flops, nbytes):
    return pl.CostEstimate(flops=int(flops), bytes_accessed=int(nbytes), transcendentals=0)


def mm(left, right, dims):
    return lax.dot_general(left, right, dims, preferred_element_type=jnp.float32)


def split(x):
    high = x.astype(jnp.bfloat16)
    return high, (x - high.astype(jnp.float32)).astype(jnp.bfloat16)


def pack_kernel(away_ref, keep_ref, away_in, keep_in, away_out, keep_out):
    for part in range(2):
        away_out[part] = away_in[:, part, :]
        keep_out[part] = keep_in[:, part, :]


def pack(traces, away, keep, width):
    slots, _, stations = traces.shape
    count = keep.shape[0]
    shape = jax.ShapeDtypeStruct((2, slots, count * width), jnp.float32)
    if width % 128:
        return tuple(
            jnp.concatenate(
                [
                    lax.dynamic_slice(traces, (0, 0, which[k] * width), (slots, 2, width))
                    for k in range(count)
                ],
                axis=2,
            ).transpose(1, 0, 2)
            for which in (away, keep)
        )
    out_spec = pl.BlockSpec((2, slots, width), lambda k, a, b: (0, 0, k))
    return pl.pallas_call(
        pack_kernel,
        grid_spec=pltpu.PrefetchScalarGridSpec(
            num_scalar_prefetch=2,
            grid=(count,),
            in_specs=[
                pl.BlockSpec((slots, 2, width), lambda k, a, b: (0, 0, a[k])),
                pl.BlockSpec((slots, 2, width), lambda k, a, b: (0, 0, b[k])),
            ],
            out_specs=[out_spec, out_spec],
        ),
        out_shape=[shape, shape],
        compiler_params=params(),
        cost_estimate=cost(0, 4 * traces.size * 4 // 2),
        name="pack",
    )(away, keep, traces, traces)


def prepare_kernel(
    keep_ref, got_ref, ids_ref, hot_ref, recorded_ref, mirrored_ref, target_ref, both_ref,
    place_ref
):
    slots = keep_ref.shape[1]
    for h, traces in enumerate((keep_ref, got_ref)):
        at = pl.ds(h * slots, slots)
        hot = hot_ref[at, :]
        own = mm(hot, recorded_ref[...], NN) > 0.5
        mir = mm(hot, mirrored_ref[...], NN) > 0.5
        place_ref[at, :] = jnp.where(ids_ref[at, :] == target_ref[...], 1.0, 0.0).astype(
            jnp.bfloat16
        )
        for part in range(2):
            high, low = split(traces[part])
            for t, piece in enumerate((high, low)):
                wide = piece.astype(jnp.float32)
                both_ref[0, 2 * part + t, at, :] = jnp.where(own, wide, 0.0).astype(jnp.bfloat16)
                both_ref[1, 2 * part + t, at, :] = jnp.where(mir, wide, 0.0).astype(jnp.bfloat16)


def prepare(keep, got, ids, hot, recorded, mirrored, target):
    _, slots, length = keep.shape
    blocks = hot.shape[1]
    tile = min(256, length)
    traces_spec = pl.BlockSpec((2, slots, tile), lambda k: (0, 0, k))
    whole = lambda shape: pl.BlockSpec(shape, lambda k: (0, 0))
    strip = lambda rows: pl.BlockSpec((rows, tile), lambda k: (0, k))
    out_spec = pl.BlockSpec((2, 4, 2 * slots, tile), lambda k: (0, 0, 0, k))
    big = jax.ShapeDtypeStruct((2, 4, 2 * slots, length), jnp.bfloat16)
    return pl.pallas_call(
        prepare_kernel,
        grid=(length // tile,),
        in_specs=[
            traces_spec,
            traces_spec,
            whole((2 * slots, 1)),
            whole((2 * slots, blocks)),
            strip(blocks),
            strip(blocks),
            strip(1),
        ],
        out_specs=[out_spec, strip(2 * slots)],
        out_shape=[big, jax.ShapeDtypeStruct((2 * slots, length), jnp.bfloat16)],
        compiler_params=params(),
        cost_estimate=cost(0, 60 * slots * length),
        name="prepare",
    )(keep, got, ids, hot, recorded, mirrored, target)


def turn(real, imag, sign):
    return jnp.concatenate([imag * (-sign), real * sign], axis=0)


def to_slots_kernel(sign, re_ref, im_ref, k_ref, place_ref, o_ref):
    real, imag = re_ref[...], im_ref[...]
    high, low = split(jnp.concatenate([real, imag], axis=0))
    high2, low2 = split(turn(real, imag, sign))
    place = place_ref[...]
    made = (
        mm(high, k_ref[0], NT)
        + mm(low, k_ref[0], NT)
        + mm(high, k_ref[1], NT)
        + mm(high2, k_ref[2], NT)
        + mm(low2, k_ref[2], NT)
        + mm(high2, k_ref[3], NT)
    )
    picked = mm(high, place, NT) + mm(low, place, NT)

    @pl.when(pl.program_id(0) == 0)
    def _():
        o_ref[0] = made
        o_ref[1] = picked

    @pl.when(pl.program_id(0) > 0)
    def _():
        o_ref[0] += made
        o_ref[1] += picked


def to_slots(real, imag, kernel, place, sign):
    cols, length = real.shape
    slots = place.shape[0]
    tile = min(512, length)
    vec = pl.BlockSpec((cols, tile), lambda k: (0, k))
    return pl.pallas_call(
        functools.partial(to_slots_kernel, sign),
        grid=(length // tile,),
        in_specs=[
            vec,
            vec,
            pl.BlockSpec((4, slots, tile), lambda k: (0, 0, k)),
            pl.BlockSpec((slots, tile), lambda k: (0, k)),
        ],
        out_specs=pl.BlockSpec((2, 2 * cols, slots), lambda k: (0, 0, 0)),
        out_shape=jax.ShapeDtypeStruct((2, 2 * cols, slots), jnp.float32),
        compiler_params=params(),
        cost_estimate=cost(32 * cols * slots * length, 10 * slots * length),
        name="to_slots",
    )(real, imag, kernel, place)


def from_slots_kernel(
    sign, mine_ref, other_ref, k_ref, place_ref, re_ref, im_ref, made, picked
):
    cols = re_ref.shape[0]
    slots = place_ref.shape[0]
    half = slots // 2

    @pl.when(pl.program_id(0) == 0)
    def _():
        def total(t):
            return mine_ref[t] + jnp.concatenate(
                [other_ref[t, :, half:], other_ref[t, :, :half]], axis=1
            )

        made[0], made[1] = split(total(0))
        vec = total(1)
        picked[0], picked[1] = split(vec)
        picked[2], picked[3] = split(turn(vec[:cols], vec[cols:], sign))

    place = place_ref[...]
    out = (
        mm(picked[0], k_ref[0], NN)
        + mm(picked[1], k_ref[0], NN)
        + mm(picked[0], k_ref[1], NN)
        + mm(picked[2], k_ref[2], NN)
        + mm(picked[3], k_ref[2], NN)
        + mm(picked[2], k_ref[3], NN)
        + mm(made[0], place, NN)
        + mm(made[1], place, NN)
    )
    re_ref[...] = out[:cols]
    im_ref[...] = out[cols:]


def from_slots(mine, other, kernel, place, sign):
    slots, length = place.shape
    cols = mine.shape[1] // 2
    tile = min(512, length)
    whole = pl.BlockSpec((2, 2 * cols, slots), lambda k: (0, 0, 0))
    vec = pl.BlockSpec((cols, tile), lambda k: (0, k))
    shape = jax.ShapeDtypeStruct((cols, length), jnp.float32)
    return pl.pallas_call(
        functools.partial(from_slots_kernel, sign),
        grid=(length // tile,),
        in_specs=[
            whole,
            whole,
            pl.BlockSpec((4, slots, tile), lambda k: (0, 0, k)),
            pl.BlockSpec((slots, tile), lambda k: (0, k)),
        ],
        out_specs=[vec, vec],
        out_shape=[shape, shape],
        scratch_shapes=[
            pltpu.VMEM((2, 2 * cols, slots), jnp.bfloat16),
            pltpu.VMEM((4, 2 * cols, slots), jnp.bfloat16),
        ],
        compiler_params=params(),
        cost_estimate=cost(32 * cols * slots * length, 10 * slots * length),
        name="from_slots",
    )(mine, other, kernel, place)


def mega_kernel(
    zs, pieces, panel_hbm, traces_hbm, weights_ref, ids_ref, hot_ref, recorded_ref,
    mirrored_ref, target_ref, field_ref, image_ref, k_hbm, place_hbm, got_hbm,
    x, v, r1, r2, r3, ug, ug_got, vecs, kbuf, pbuf, tbuf, stage,
    ag_send, ag_recv, rs_send, rs_recv, ug_sem, k_sem, ready,
    panel_sem, swap_send, swap_recv, in_sem, out_sem, field_send, field_recv
):
    z, core, j = (lax.axis_index(name) for name in AXES)
    cols = 4
    step_cols, width = x.shape[3], x.shape[4]
    slots = ug.shape[2]
    half = slots // 2
    tile = 2 * width
    tiles = cols * zs // 2
    near_x = (z, core, j + 1 - 2 * (j % 2))
    near_y = (z, core, (j + 2) % 4)
    other = (z, 1 - core, j)

    def along(d):
        return ((z + d) % zs, core, j)

    first_to, second_to = (near_x, near_y), (near_y, near_x)
    first_at, second_at = (1, 2), (2, 1)
    peers = [near_x, near_y, other] + [along(d) for d in range(1, zs)]
    rows = 2 * zs
    me = (z * 2 + core) * cols + j
    block = j * rows + z * 2 + core
    goal = (block // cols // 2, block // cols % 2, block % cols)
    origin = (me % rows // 2, me % rows % 2, me // rows)
    stays = block == me

    def remote(src, dst, send, recv, to):
        return pltpu.make_async_remote_copy(
            src_ref=src, dst_ref=dst, send_sem=send, recv_sem=recv, device_id=to,
            device_id_type=pl.DeviceIdType.MESH,
        )

    def spread(h, kind, p, d):
        if kind == 0:
            src, dst, to = 0, d, ((z + zs - d) % zs, core, j)
        elif kind == 1:
            src, dst, to = d, first_at[p] * zs + d, first_to[p]
        elif kind == 2:
            src, dst, to = d, second_at[p] * zs + d, second_to[p]
        else:
            src, dst, to = first_at[p] * zs + d, 3 * zs + d, second_to[p]
        at = (kind * 2 + p) * zs + d
        return remote(
            x.at[h, p, src], x.at[h, p, dst], ag_send.at[h, at], ag_recv.at[h, at], to
        )

    def spread_line(h):
        for p in range(2):
            for d in range(1, zs):
                spread(h, 0, p, d).start()
        for p in range(2):
            spread(h, 1, p, 0).start()
            spread(h, 2, p, 0).start()

    def spread_more(h, d):
        for p in range(2):
            spread(h, 0, p, d).wait_recv()
            spread(h, 1, p, d).start()
            spread(h, 2, p, d).start()

    def spread_last(h, d):
        for p in range(2):
            spread(h, 1, p, d).wait_recv()
            spread(h, 3, p, d).start()

    def spread_end(h):
        for p in range(2):
            for d in range(zs):
                if d:
                    spread(h, 0, p, d).wait_send()
                spread(h, 1, p, d).wait_send()
                spread(h, 2, p, d).wait()
                spread(h, 3, p, d).wait()

    def sum1(par, p, e, d):
        src = (first_at[p] if e == 0 else 3) * zs + d
        at = (p * 2 + e) * zs + d
        return remote(
            v.at[par, p, src], r1.at[p, e, d], rs_send.at[at], rs_recv.at[at], first_to[p]
        )

    def sum2(par, p, d):
        at = (4 + p) * zs + d
        return remote(
            v.at[par, p, second_at[p] * zs + d], r2.at[p, d], rs_send.at[at], rs_recv.at[at],
            second_to[p],
        )

    def sum3(par, p, d):
        at = (6 + p) * zs + d
        return remote(
            v.at[par, p, d], r3.at[p, d], rs_send.at[at], rs_recv.at[at], along(d)
        )

    def sum_first(par):
        for d in range(zs):
            for p in range(2):
                for e in range(2):
                    sum1(par, p, e, d).start()

    def sum_second(par, d):
        for p in range(2):
            for e in range(2):
                sum1(par, p, e, d).wait_recv()
            at = second_at[p] * zs + d
            v[par, p, at] += r1[p, 1, d]
            sum2(par, p, d).start()
            v[par, p, d] += r1[p, 0, d]

    def sum_third(par, d):
        for p in range(2):
            sum2(par, p, d).wait_recv()
            v[par, p, d] += r2[p, d]

            @pl.when(d > 0)
            def _():
                sum3(par, p, d).start()

    def deliver(h, action):
        @pl.when(stays)
        def _():
            getattr(
                pltpu.make_async_copy(stage.at[h], field_ref.at[h], field_send.at[h]), action
            )()

        @pl.when(jnp.logical_not(stays))
        def _():
            getattr(
                remote(
                    stage.at[h], field_ref.at[h], field_send.at[h], field_recv.at[h], goal
                ),
                action,
            )()

    def sum_end(par, h, phase):
        for p in range(2):
            out = v[par, p, 0]
            for d in range(1, zs):
                sum3(par, p, d).wait_recv()
                out = out + r3[p, d]

            @pl.when(phase == 0)
            def _():
                stage[h, p] = out
                x[h, p, 0] = out * weights_ref[...]

            @pl.when(phase == 1)
            def _():
                image_ref[h, p] = out

        @pl.when(phase == 0)
        def _():
            deliver(h, "start")

        for p in range(2):
            for d in range(zs):
                for e in range(2):
                    sum1(par, p, e, d).wait_send()
                sum2(par, p, d).wait_send()
                if d:
                    sum3(par, p, d).wait_send()

    def fetch(which, k, buf):
        at = pl.ds(pl.multiple_of(k * tile, tile), tile)
        return (
            pltpu.make_async_copy(k_hbm.at[which, :, :, at], kbuf.at[buf], k_sem.at[buf, 0]),
            pltpu.make_async_copy(place_hbm.at[:, at], pbuf.at[buf], k_sem.at[buf, 1]),
        )

    def fetch_start(which, k, buf):
        for copy in fetch(which, k, buf):
            copy.start()

    def fetch_wait(which, k, buf):
        for copy in fetch(which, k, buf):
            copy.wait()

    def slots_step(h, k, buf, sign):
        real = jnp.concatenate([x[h, 0, 2 * k], x[h, 0, 2 * k + 1]], axis=1)
        imag = jnp.concatenate([x[h, 1, 2 * k], x[h, 1, 2 * k + 1]], axis=1)
        high, low = split(jnp.concatenate([real, imag], axis=0))
        high2, low2 = split(jnp.concatenate([imag * (-sign), real * sign], axis=0))
        place = pbuf[buf]
        ug[0] += (
            mm(high, kbuf[buf, 0], NT)
            + mm(low, kbuf[buf, 0], NT)
            + mm(high, kbuf[buf, 1], NT)
            + mm(high2, kbuf[buf, 2], NT)
            + mm(low2, kbuf[buf, 2], NT)
            + mm(high2, kbuf[buf, 3], NT)
        )
        ug[1] += mm(high, place, NT) + mm(low, place, NT)

    def vecs_make(sign):
        def total(t):
            return ug[t] + jnp.concatenate([ug_got[t, :, half:], ug_got[t, :, :half]], axis=1)

        vecs[0], vecs[1] = split(total(0))
        vec = total(1)
        vecs[2], vecs[3] = split(vec)
        vecs[4], vecs[5] = split(
            jnp.concatenate([vec[step_cols:] * (-sign), vec[:step_cols] * sign], axis=0)
        )

    def sources_step(par, k, buf):
        place = pbuf[buf]
        out = (
            mm(vecs[2], kbuf[buf, 0], NN)
            + mm(vecs[3], kbuf[buf, 0], NN)
            + mm(vecs[2], kbuf[buf, 1], NN)
            + mm(vecs[4], kbuf[buf, 2], NN)
            + mm(vecs[5], kbuf[buf, 2], NN)
            + mm(vecs[4], kbuf[buf, 3], NN)
            + mm(vecs[0], place, NN)
            + mm(vecs[1], place, NN)
        )
        for p in range(2):
            for e in range(2):
                v[par, p, 2 * k + e] = out[
                    p * step_cols : (p + 1) * step_cols, e * width : (e + 1) * width
                ]

    def receivers(k):
        q, d = k // zs, k % zs
        col = (j + q) % 2 + 2 * ((j // 2 + q // 2) % 2)
        return col * rows + (z + d) % zs * 2

    def lanes(at):
        return pl.ds(pl.multiple_of(at * width, width), width)

    def swap(k):
        return remote(
            traces_hbm.at[:, :, lanes(receivers(k) + 1 - core)], got_hbm.at[k],
            swap_send.at[k], swap_recv.at[k], other,
        )

    def load(k, buf):
        return (
            pltpu.make_async_copy(
                traces_hbm.at[:, :, lanes(receivers(k) + core)], tbuf.at[buf, 0],
                in_sem.at[buf, 0],
            ),
            pltpu.make_async_copy(got_hbm.at[k], tbuf.at[buf, 1], in_sem.at[buf, 1]),
        )

    def load_start(k, buf):
        swap(k).wait_recv()
        for copy in load(k, buf):
            copy.start()

    def store(k, buf):
        return [
            pltpu.make_async_copy(
                kbuf.at[buf, :, :, pl.ds(which * width, width)],
                k_hbm.at[which, :, :, lanes(k)],
                out_sem.at[buf, which],
            )
            for which in range(2)
        ] + [
            pltpu.make_async_copy(
                pbuf.at[buf, :, pl.ds(0, width)], place_hbm.at[:, lanes(k)], out_sem.at[buf, 2]
            )
        ]

    def prepare_step(k, buf):
        part_slots = tbuf.shape[2]
        at = lanes(k)
        for half_at in range(2):
            these = pl.ds(half_at * part_slots, part_slots)
            hot = hot_ref[these, :]
            own = mm(hot, recorded_ref[:, at], NN) > 0.5
            mir = mm(hot, mirrored_ref[:, at], NN) > 0.5
            pbuf[buf, these, pl.ds(0, width)] = jnp.where(
                ids_ref[these, :] == target_ref[:, at], 1.0, 0.0
            ).astype(jnp.bfloat16)
            for part in range(2):
                high, low = split(tbuf[buf, half_at, :, part, :])
                for n, piece in enumerate((high, low)):
                    wide = piece.astype(jnp.float32)
                    for which, mask in enumerate((own, mir)):
                        kbuf[buf, 2 * part + n, these, pl.ds(which * width, width)] = jnp.where(
                            mask, wide, 0.0
                        ).astype(jnp.bfloat16)

    def loop(low, high, body):
        def step(i, carry):
            body(i)
            return carry

        lax.fori_loop(low, high, step, 0)

    barrier = pltpu.get_barrier_semaphore()
    for peer in peers:
        pl.semaphore_signal(
            barrier, inc=1, device_id=peer, device_id_type=pl.DeviceIdType.MESH
        )

    @pl.when(jnp.logical_not(stays))
    def _():
        for peer in (goal, origin):
            pl.semaphore_signal(
                barrier, inc=1, device_id=peer, device_id_type=pl.DeviceIdType.MESH
            )

    def own_piece(h, p):
        return pltpu.make_async_copy(
            panel_hbm.at[p, h], x.at[h, p, 0], panel_sem.at[h * 2 + p]
        )

    for h in range(pieces):
        for p in range(2):
            own_piece(h, p).start()
    for h in range(pieces):
        for p in range(2):
            own_piece(h, p).wait()

    @pl.when(stays)
    def _():
        pl.semaphore_wait(barrier, len(peers))

    @pl.when(jnp.logical_not(stays))
    def _():
        pl.semaphore_wait(barrier, len(peers) + 2)

    count = cols * zs
    loop(0, 2, spread_line)
    loop(0, count, lambda k: swap(k).start())
    load_start(0, 0)

    def prepare_pair(i):
        for e in range(2):
            k = 2 * i + e
            if e == 0:
                load_start(k + 1, 1)
            else:

                @pl.when(k + 1 < count)
                def _():
                    load_start(k + 1, 0)

            for copy in load(k, e):
                copy.wait()

            @pl.when(i > 0)
            def _():
                for copy in store(k - 2, e):
                    copy.wait()

            prepare_step(k, e)
            for copy in store(k, e):
                copy.start()
        h, d = i // zs, i % zs

        @pl.when(d > 0)
        def _():
            spread_more(h, d)

    loop(0, count // 2, prepare_pair)
    for e in range(2):
        for copy in store(count - 2 + e, e):
            copy.wait()
    loop(0, count, lambda k: swap(k).wait_send())
    fetch_start(0, 0, 0)
    loop(0, zs, lambda d: spread_last(0, d))

    def turn_of(t):
        for n, peer in enumerate(peers):
            pl.semaphore_signal(
                ready.at[n], inc=1, device_id=peer, device_id_type=pl.DeviceIdType.MESH
            )
        for n in range(len(peers)):
            pl.semaphore_wait(ready.at[n], 1)
        h, phase, par = t % pieces, t // pieces, t % 2
        sign = (1 - 2 * phase).astype(jnp.float32)
        computes = t < 2 * pieces
        sums = t > 0
        spreads = t < pieces + 2
        h_sum, phase_sum, par_sum = (t + pieces - 1) % pieces, (t - 1) // pieces, (t + 1) % 2
        h_spread = (t + pieces - 2) % pieces
        lasts, h_last = t < pieces + 3, (t + 1) % pieces

        @pl.when(sums)
        def _():
            sum_first(par_sum)

        @pl.when(spreads)
        def _():
            spread_line(h_spread)

        @pl.when(computes)
        def _():
            spread_end(h)
            ug[...] = jnp.zeros_like(ug)

        def first_half(d):
            @pl.when(computes)
            def _():
                for e in range(2):
                    k = 2 * d + e
                    fetch_wait(phase, k, e)
                    if e == 0:
                        fetch_start(phase, k + 1, 1)
                    else:
                        more = k + 1 < tiles

                        @pl.when(more)
                        def _():
                            fetch_start(phase, k + 1, 0)

                        @pl.when(jnp.logical_not(more))
                        def _():
                            fetch_start(1 - phase, 0, 0)

                    slots_step(h, k, e, sign)

            @pl.when(sums)
            def _():
                sum_second(par_sum, d)

            @pl.when(lasts)
            def _():
                spread_last(h_last, d)

        loop(0, zs, first_half)

        @pl.when(computes)
        def _():
            swap = remote(ug, ug_got, ug_sem.at[0], ug_sem.at[1], other)
            swap.start()
            swap.wait()
            vecs_make(sign)

        def second_half(d):
            @pl.when(computes)
            def _():
                for e in range(2):
                    k = 2 * d + e
                    fetch_wait(1 - phase, k, e)
                    if e == 0:
                        fetch_start(1 - phase, k + 1, 1)
                    else:

                        @pl.when(k + 1 < tiles)
                        def _():
                            fetch_start(1 - phase, k + 1, 0)

                        @pl.when(jnp.logical_and(k + 1 == tiles, t + 1 < 2 * pieces))
                        def _():
                            fetch_start((t + 1) // pieces, 0, 0)

                    sources_step(par, k, e)

            @pl.when(sums)
            def _():
                sum_third(par_sum, d)

            @pl.when(jnp.logical_and(spreads, d > 0))
            def _():
                spread_more(h_spread, d)

        loop(0, zs, second_half)

        @pl.when(sums)
        def _():
            sum_end(par_sum, h_sum, phase_sum)

    loop(0, 2 * pieces + 1, turn_of)
    loop(0, pieces, lambda h: deliver(h, "wait"))


def mega(panel, traces, weights, ids, hot, recorded, mirrored, target, zs, pieces):
    _, focus, width = panel.shape
    part_slots = traces.shape[0]
    slots = 2 * part_slots
    step = focus // pieces
    blocks = 4 * zs
    length = blocks * width
    panel = panel.reshape(2, pieces, step, width)
    vmem = pl.BlockSpec(memory_space=pltpu.VMEM)
    hbm = pl.BlockSpec(memory_space=pl.ANY)
    f32, b16 = jnp.float32, jnp.bfloat16
    dma = pltpu.SemaphoreType.DMA
    shape = jax.ShapeDtypeStruct((pieces, 2, step, width), f32)
    return pl.pallas_call(
        functools.partial(mega_kernel, zs, pieces),
        in_specs=[hbm, hbm] + [vmem] * 6,
        out_specs=[vmem, vmem, hbm, hbm, hbm],
        out_shape=[
            shape,
            shape,
            jax.ShapeDtypeStruct((2, 4, slots, length), b16),
            jax.ShapeDtypeStruct((slots, length), b16),
            jax.ShapeDtypeStruct((blocks, part_slots, 2, width), f32),
        ],
        scratch_shapes=[
            pltpu.VMEM((pieces, 2, blocks, step, width), f32),
            pltpu.VMEM((2, 2, blocks, step, width), f32),
            pltpu.VMEM((2, 2, zs, step, width), f32),
            pltpu.VMEM((2, zs, step, width), f32),
            pltpu.VMEM((2, zs, step, width), f32),
            pltpu.VMEM((2, 2 * step, slots), f32),
            pltpu.VMEM((2, 2 * step, slots), f32),
            pltpu.VMEM((6, 2 * step, slots), b16),
            pltpu.VMEM((2, 4, slots, 2 * width), b16),
            pltpu.VMEM((2, slots, 2 * width), b16),
            pltpu.VMEM((2, 2, part_slots, 2, width), f32),
            pltpu.VMEM((pieces, 2, step, width), f32),
            dma((pieces, 8 * zs)),
            dma((pieces, 8 * zs)),
            dma((8 * zs,)),
            dma((8 * zs,)),
            dma((2,)),
            dma((2, 2)),
            pltpu.SemaphoreType.REGULAR((zs + 2,)),
            dma((2 * pieces,)),
            dma((blocks,)),
            dma((blocks,)),
            dma((2, 2)),
            dma((2, 3)),
            dma((pieces,)),
            dma((pieces,)),
        ],
        compiler_params=pltpu.CompilerParams(
            collective_id=0, has_side_effects=True, vmem_limit_bytes=MEGA_VMEM
        ),
        name="products",
    )(panel, traces, weights, ids, hot, recorded, mirrored, target)[:2]


def lookup(bins, table):
    matches = bins[:, None] == jnp.arange(table.shape[0], dtype=jnp.int32)[None, :]
    return jnp.sum(jnp.where(matches, table[None, :], 0.0), axis=1)


def local(
    zs, cols, shot_traces, shot_ids, shot_counts, missing_blocks, weight_bins, weight_table,
    focus_panel
):
    slots, _, stations = shot_traces.shape
    focus = focus_panel.shape[2]
    width = focus_panel.shape[1]
    rows = 2 * zs
    z, core, j = (lax.axis_index(name) for name in AXES)
    bits = [1 << b for b in range(cols.bit_length() - 1)]
    assert 1 << len(bits) == cols

    def device(a, c, b):
        return (a * 2 + c) * cols + b

    everyone = [(a, c, b) for a in range(zs) for c in range(2) for b in range(cols)]

    def send(x, target):
        return lax.ppermute(x, AXES, [(device(*d), device(*target(*d))) for d in everyone])

    def across_core(x):
        return send(x, lambda a, c, b: (a, 1 - c, b))

    def gather(piece, order):
        group = [piece] + [
            send(piece, lambda a, c, b, d=d: ((a - d) % zs, c, b)) for d in range(1, zs)
        ]
        size = zs * width
        groups = {0: jnp.concatenate(group, axis=1)}
        for bit in order:
            keys = sorted(groups)
            got = send(
                jnp.concatenate([groups[k] for k in keys], axis=1),
                lambda a, c, b: (a, c, b ^ bit),
            )
            for n, k in enumerate(keys):
                groups[k | bit] = got[:, n * size : (n + 1) * size]
        return jnp.concatenate([groups[k] for k in range(cols)], axis=1)

    def scatter(total, order):
        size = zs * width
        groups = {k: total[:, k * size : (k + 1) * size] for k in range(cols)}
        for bit in order:
            away = sorted(k for k in groups if k & bit)
            got = send(
                jnp.concatenate([groups[k] for k in away], axis=1),
                lambda a, c, b: (a, c, b ^ bit),
            )
            for n, k in enumerate(away):
                groups[k ^ bit] = groups[k ^ bit] + got[:, n * size : (n + 1) * size]
                del groups[k]
        line = groups[0]
        out = line[:, :width]
        for d in range(1, zs):
            out = out + send(
                line[:, d * width : (d + 1) * width],
                lambda a, c, b: ((a + d) % zs, c, b),
            )
        return out

    order_re, order_im = bits, bits[::-1]

    rel = [(q, d) for q in range(cols) for d in range(zs)]
    places = jnp.stack(
        [lax.bitwise_xor(j, jnp.int32(q)) * rows + lax.rem(z + d, zs) * 2 for q, d in rel]
    ).astype(jnp.int32)
    keep_at, away_at = places + core, places + 1 - core
    counted = jnp.where(jnp.arange(slots, dtype=jnp.int32) < shot_counts[0], shot_ids, -1)
    ids = jnp.concatenate([counted, across_core(counted)])[:, None]
    down, over = missing_blocks.shape
    missing = lax.dynamic_update_slice(
        jnp.zeros((rows * down, cols * over), jnp.int32),
        missing_blocks,
        ((z * 2 + core) * down, j * over),
    )
    assert zs & (zs - 1) == 0
    missing = missing + across_core(missing)
    for bit in bits:
        missing = missing + send(missing, lambda a, c, b: (a, c, b ^ bit))
    for bit in (1 << n for n in range(zs.bit_length() - 1)):
        missing = missing + send(missing, lambda a, c, b: (a ^ bit, c, b))
    missing = missing.astype(jnp.bfloat16)
    blocks = missing.shape[0]
    side = stations // blocks
    hot = jnp.where(ids // side == jnp.arange(blocks, dtype=jnp.int32)[None, :], 1.0, 0.0)
    hot = jnp.where(ids >= 0, hot, 0.0).astype(jnp.bfloat16)
    target = (keep_at[:, None] * width + jnp.arange(width, dtype=jnp.int32)[None, :]).reshape(1, -1)
    spread = jnp.where(
        target // side == jnp.arange(blocks, dtype=jnp.int32)[:, None], 1.0, 0.0
    ).astype(jnp.bfloat16)
    recorded = mm(1 - missing, spread, NN).astype(jnp.bfloat16)
    mirrored = mm(missing.T, spread, NN).astype(jnp.bfloat16)

    pairs = []
    for n in range(rows * cols):
        i, b = n % rows, n // rows
        pairs.append((n, i * cols + b))
    bins = lax.ppermute(weight_bins, AXES, pairs)
    weights = lookup(bins, weight_table)[None, :]
    back = [(b, a) for a, b in pairs]

    def product(real, imag, first, second, sign):
        real, imag = gather(real, order_re), gather(imag, order_im)
        mine = to_slots(real, imag, first, place, sign)
        real, imag = from_slots(mine, across_core(mine), second, place, sign)
        return scatter(real, order_re), scatter(imag, order_im)

    panel = focus_panel.transpose(0, 2, 1)
    if cols == 4 and width % 128 == 0:
        outs = mega(
            panel, shot_traces, weights, ids, hot, recorded, mirrored, target, zs, TURNS
        )
        return tuple(out.transpose(1, 3, 0, 2).reshape(2, width, focus) for out in outs)
    step = focus // PIECES
    away, keep = pack(shot_traces, away_at, keep_at, width)
    got = across_core(away)
    kernels, place = prepare(keep, got, ids, hot, recorded, mirrored, target)
    own, mir = kernels[0], kernels[1]
    fields, images = [], []
    for h in range(PIECES):
        at = slice(h * step, (h + 1) * step)
        real, imag = product(panel[0, at], panel[1, at], own, mir, 1)
        fields.append(jnp.stack([real, imag]))
        real, imag = product(real * weights, imag * weights, mir, own, -1)
        images.append(jnp.stack([real, imag]))
    field = lax.ppermute(jnp.concatenate(fields, axis=1), AXES, back)
    return field.transpose(0, 2, 1), jnp.concatenate(images, axis=1).transpose(0, 2, 1)


def solution(mesh):
    rows, cols = mesh.shape["row"], mesh.shape["col"]
    zs = rows // 2
    split_mesh = Mesh(mesh.devices.reshape(zs, 2, cols), AXES)
    rowwise = ("z", "core", "col")
    colwise = ("col", "z", "core")
    placed = (
        P(rowwise, None, None),
        P(rowwise),
        P(rowwise),
        P(("z", "core"), "col"),
        P(rowwise),
        P(),
        P(None, colwise, None),
    )
    return jax.shard_map(
        functools.partial(local, zs, cols),
        mesh=split_mesh,
        in_specs=placed,
        out_specs=(P(None, rowwise, None), P(None, colwise, None)),
        check_vma=False,
    )
```

```python
import functools

import jax
import jax.numpy as jnp
from jax import lax
from jax.experimental import pallas as pl
from jax.experimental.pallas import tpu as pltpu
from jax.sharding import Mesh
from jax.sharding import PartitionSpec as P

AXES = ("z", "core", "col")
PIECES = 2
VMEM = 56 * 1024 * 1024
MEGA_VMEM = 60 * 1024 * 1024
TURNS = 4
NT = (((1,), (1,)), ((), ()))
NN = (((1,), (0,)), ((), ()))


def params():
    return pltpu.CompilerParams(vmem_limit_bytes=VMEM)


def cost(flops, nbytes):
    return pl.CostEstimate(flops=int(flops), bytes_accessed=int(nbytes), transcendentals=0)


def mm(left, right, dims):
    return lax.dot_general(left, right, dims, preferred_element_type=jnp.float32)


def split(x):
    high = x.astype(jnp.bfloat16)
    return high, (x - high.astype(jnp.float32)).astype(jnp.bfloat16)


def pack_kernel(away_ref, keep_ref, away_in, keep_in, away_out, keep_out):
    for part in range(2):
        away_out[part] = away_in[:, part, :]
        keep_out[part] = keep_in[:, part, :]


def pack(traces, away, keep, width):
    slots, _, stations = traces.shape
    count = keep.shape[0]
    shape = jax.ShapeDtypeStruct((2, slots, count * width), jnp.float32)
    if width % 128:
        return tuple(
            jnp.concatenate(
                [
                    lax.dynamic_slice(traces, (0, 0, which[k] * width), (slots, 2, width))
                    for k in range(count)
                ],
                axis=2,
            ).transpose(1, 0, 2)
            for which in (away, keep)
        )
    out_spec = pl.BlockSpec((2, slots, width), lambda k, a, b: (0, 0, k))
    return pl.pallas_call(
        pack_kernel,
        grid_spec=pltpu.PrefetchScalarGridSpec(
            num_scalar_prefetch=2,
            grid=(count,),
            in_specs=[
                pl.BlockSpec((slots, 2, width), lambda k, a, b: (0, 0, a[k])),
                pl.BlockSpec((slots, 2, width), lambda k, a, b: (0, 0, b[k])),
            ],
            out_specs=[out_spec, out_spec],
        ),
        out_shape=[shape, shape],
        compiler_params=params(),
        cost_estimate=cost(0, 4 * traces.size * 4 // 2),
        name="pack",
    )(away, keep, traces, traces)


def prepare_kernel(
    keep_ref, got_ref, ids_ref, hot_ref, recorded_ref, mirrored_ref, target_ref, both_ref,
    place_ref
):
    slots = keep_ref.shape[1]
    for h, traces in enumerate((keep_ref, got_ref)):
        at = pl.ds(h * slots, slots)
        hot = hot_ref[at, :]
        own = mm(hot, recorded_ref[...], NN) > 0.5
        mir = mm(hot, mirrored_ref[...], NN) > 0.5
        place_ref[at, :] = jnp.where(ids_ref[at, :] == target_ref[...], 1.0, 0.0).astype(
            jnp.bfloat16
        )
        for part in range(2):
            high, low = split(traces[part])
            for t, piece in enumerate((high, low)):
                wide = piece.astype(jnp.float32)
                both_ref[0, 2 * part + t, at, :] = jnp.where(own, wide, 0.0).astype(jnp.bfloat16)
                both_ref[1, 2 * part + t, at, :] = jnp.where(mir, wide, 0.0).astype(jnp.bfloat16)


def prepare(keep, got, ids, hot, recorded, mirrored, target):
    _, slots, length = keep.shape
    blocks = hot.shape[1]
    tile = min(256, length)
    traces_spec = pl.BlockSpec((2, slots, tile), lambda k: (0, 0, k))
    whole = lambda shape: pl.BlockSpec(shape, lambda k: (0, 0))
    strip = lambda rows: pl.BlockSpec((rows, tile), lambda k: (0, k))
    out_spec = pl.BlockSpec((2, 4, 2 * slots, tile), lambda k: (0, 0, 0, k))
    big = jax.ShapeDtypeStruct((2, 4, 2 * slots, length), jnp.bfloat16)
    return pl.pallas_call(
        prepare_kernel,
        grid=(length // tile,),
        in_specs=[
            traces_spec,
            traces_spec,
            whole((2 * slots, 1)),
            whole((2 * slots, blocks)),
            strip(blocks),
            strip(blocks),
            strip(1),
        ],
        out_specs=[out_spec, strip(2 * slots)],
        out_shape=[big, jax.ShapeDtypeStruct((2 * slots, length), jnp.bfloat16)],
        compiler_params=params(),
        cost_estimate=cost(0, 60 * slots * length),
        name="prepare",
    )(keep, got, ids, hot, recorded, mirrored, target)


def turn(real, imag, sign):
    return jnp.concatenate([imag * (-sign), real * sign], axis=0)


def to_slots_kernel(sign, re_ref, im_ref, k_ref, place_ref, o_ref):
    real, imag = re_ref[...], im_ref[...]
    high, low = split(jnp.concatenate([real, imag], axis=0))
    high2, low2 = split(turn(real, imag, sign))
    place = place_ref[...]
    made = (
        mm(high, k_ref[0], NT)
        + mm(low, k_ref[0], NT)
        + mm(high, k_ref[1], NT)
        + mm(high2, k_ref[2], NT)
        + mm(low2, k_ref[2], NT)
        + mm(high2, k_ref[3], NT)
    )
    picked = mm(high, place, NT) + mm(low, place, NT)

    @pl.when(pl.program_id(0) == 0)
    def _():
        o_ref[0] = made
        o_ref[1] = picked

    @pl.when(pl.program_id(0) > 0)
    def _():
        o_ref[0] += made
        o_ref[1] += picked


def to_slots(real, imag, kernel, place, sign):
    cols, length = real.shape
    slots = place.shape[0]
    tile = min(512, length)
    vec = pl.BlockSpec((cols, tile), lambda k: (0, k))
    return pl.pallas_call(
        functools.partial(to_slots_kernel, sign),
        grid=(length // tile,),
        in_specs=[
            vec,
            vec,
            pl.BlockSpec((4, slots, tile), lambda k: (0, 0, k)),
            pl.BlockSpec((slots, tile), lambda k: (0, k)),
        ],
        out_specs=pl.BlockSpec((2, 2 * cols, slots), lambda k: (0, 0, 0)),
        out_shape=jax.ShapeDtypeStruct((2, 2 * cols, slots), jnp.float32),
        compiler_params=params(),
        cost_estimate=cost(32 * cols * slots * length, 10 * slots * length),
        name="to_slots",
    )(real, imag, kernel, place)


def from_slots_kernel(
    sign, mine_ref, other_ref, k_ref, place_ref, re_ref, im_ref, made, picked
):
    cols = re_ref.shape[0]
    slots = place_ref.shape[0]
    half = slots // 2

    @pl.when(pl.program_id(0) == 0)
    def _():
        def total(t):
            return mine_ref[t] + jnp.concatenate(
                [other_ref[t, :, half:], other_ref[t, :, :half]], axis=1
            )

        made[0], made[1] = split(total(0))
        vec = total(1)
        picked[0], picked[1] = split(vec)
        picked[2], picked[3] = split(turn(vec[:cols], vec[cols:], sign))

    place = place_ref[...]
    out = (
        mm(picked[0], k_ref[0], NN)
        + mm(picked[1], k_ref[0], NN)
        + mm(picked[0], k_ref[1], NN)
        + mm(picked[2], k_ref[2], NN)
        + mm(picked[3], k_ref[2], NN)
        + mm(picked[2], k_ref[3], NN)
        + mm(made[0], place, NN)
        + mm(made[1], place, NN)
    )
    re_ref[...] = out[:cols]
    im_ref[...] = out[cols:]


def from_slots(mine, other, kernel, place, sign):
    slots, length = place.shape
    cols = mine.shape[1] // 2
    tile = min(512, length)
    whole = pl.BlockSpec((2, 2 * cols, slots), lambda k: (0, 0, 0))
    vec = pl.BlockSpec((cols, tile), lambda k: (0, k))
    shape = jax.ShapeDtypeStruct((cols, length), jnp.float32)
    return pl.pallas_call(
        functools.partial(from_slots_kernel, sign),
        grid=(length // tile,),
        in_specs=[
            whole,
            whole,
            pl.BlockSpec((4, slots, tile), lambda k: (0, 0, k)),
            pl.BlockSpec((slots, tile), lambda k: (0, k)),
        ],
        out_specs=[vec, vec],
        out_shape=[shape, shape],
        scratch_shapes=[
            pltpu.VMEM((2, 2 * cols, slots), jnp.bfloat16),
            pltpu.VMEM((4, 2 * cols, slots), jnp.bfloat16),
        ],
        compiler_params=params(),
        cost_estimate=cost(32 * cols * slots * length, 10 * slots * length),
        name="from_slots",
    )(mine, other, kernel, place)


def mega_kernel(
    zs, pieces, panel_hbm, traces_hbm, weights_ref, ids_ref, hot_ref, recorded_ref,
    mirrored_ref, target_ref, field_ref, image_ref, k_hbm, place_hbm, got_hbm,
    x, v, r1, r2, r3, ug, ug_got, vecs, kbuf, pbuf, tbuf, stage,
    ag_send, ag_recv, rs_send, rs_recv, ug_sem, k_sem, ready,
    panel_sem, swap_send, swap_recv, in_sem, out_sem, field_send, field_recv
):
    z, core, j = (lax.axis_index(name) for name in AXES)
    cols = 4
    step_cols, width = x.shape[3], x.shape[4]
    slots = ug.shape[2]
    half = slots // 2
    tile = 2 * width
    tiles = cols * zs // 2
    near_x = (z, core, j + 1 - 2 * (j % 2))
    near_y = (z, core, (j + 2) % 4)
    other = (z, 1 - core, j)

    def along(d):
        return ((z + d) % zs, core, j)

    first_to, second_to = (near_x, near_y), (near_y, near_x)
    first_at, second_at = (1, 2), (2, 1)
    peers = [near_x, near_y, other] + [along(d) for d in range(1, zs)]
    rows = 2 * zs
    me = (z * 2 + core) * cols + j
    block = j * rows + z * 2 + core
    goal = (block // cols // 2, block // cols % 2, block % cols)
    origin = (me % rows // 2, me % rows % 2, me // rows)
    stays = block == me

    def remote(src, dst, send, recv, to):
        return pltpu.make_async_remote_copy(
            src_ref=src, dst_ref=dst, send_sem=send, recv_sem=recv, device_id=to,
            device_id_type=pl.DeviceIdType.MESH,
        )

    def spread(h, kind, p, d):
        if kind == 0:
            src, dst, to = 0, d, ((z + zs - d) % zs, core, j)
        elif kind == 1:
            src, dst, to = d, first_at[p] * zs + d, first_to[p]
        elif kind == 2:
            src, dst, to = d, second_at[p] * zs + d, second_to[p]
        else:
            src, dst, to = first_at[p] * zs + d, 3 * zs + d, second_to[p]
        at = (kind * 2 + p) * zs + d
        return remote(
            x.at[h, p, src], x.at[h, p, dst], ag_send.at[h, at], ag_recv.at[h, at], to
        )

    def spread_line(h):
        for p in range(2):
            for d in range(1, zs):
                spread(h, 0, p, d).start()
        for p in range(2):
            spread(h, 1, p, 0).start()
            spread(h, 2, p, 0).start()

    def spread_more(h, d):
        for p in range(2):
            spread(h, 0, p, d).wait_recv()
            spread(h, 1, p, d).start()
            spread(h, 2, p, d).start()

    def spread_last(h, d):
        for p in range(2):
            spread(h, 1, p, d).wait_recv()
            spread(h, 3, p, d).start()

    def spread_end(h):
        for p in range(2):
            for d in range(zs):
                if d:
                    spread(h, 0, p, d).wait_send()
                spread(h, 1, p, d).wait_send()
                spread(h, 2, p, d).wait()
                spread(h, 3, p, d).wait()

    def sum1(par, p, e, d):
        src = (first_at[p] if e == 0 else 3) * zs + d
        at = (p * 2 + e) * zs + d
        return remote(
            v.at[par, p, src], r1.at[p, e, d], rs_send.at[at], rs_recv.at[at], first_to[p]
        )

    def sum2(par, p, d):
        at = (4 + p) * zs + d
        return remote(
            v.at[par, p, second_at[p] * zs + d], r2.at[p, d], rs_send.at[at], rs_recv.at[at],
            second_to[p],
        )

    def sum3(par, p, d):
        at = (6 + p) * zs + d
        return remote(
            v.at[par, p, d], r3.at[p, d], rs_send.at[at], rs_recv.at[at], along(d)
        )

    def sum_first(par):
        for d in range(zs):
            for p in range(2):
                for e in range(2):
                    sum1(par, p, e, d).start()

    def sum_second(par, d):
        for p in range(2):
            for e in range(2):
                sum1(par, p, e, d).wait_recv()
            at = second_at[p] * zs + d
            v[par, p, at] += r1[p, 1, d]
            sum2(par, p, d).start()
            v[par, p, d] += r1[p, 0, d]

    def sum_third(par, d):
        for p in range(2):
            sum2(par, p, d).wait_recv()
            v[par, p, d] += r2[p, d]

            @pl.when(d > 0)
            def _():
                sum3(par, p, d).start()

    def deliver(h, action):
        @pl.when(stays)
        def _():
            getattr(
                pltpu.make_async_copy(stage.at[h], field_ref.at[h], field_send.at[h]), action
            )()

        @pl.when(jnp.logical_not(stays))
        def _():
            getattr(
                remote(
                    stage.at[h], field_ref.at[h], field_send.at[h], field_recv.at[h], goal
                ),
                action,
            )()

    def sum_end(par, h, phase):
        for p in range(2):
            out = v[par, p, 0]
            for d in range(1, zs):
                sum3(par, p, d).wait_recv()
                out = out + r3[p, d]

            @pl.when(phase == 0)
            def _():
                stage[h, p] = out
                x[h, p, 0] = out * weights_ref[...]

            @pl.when(phase == 1)
            def _():
                image_ref[h, p] = out

        @pl.when(phase == 0)
        def _():
            deliver(h, "start")

        for p in range(2):
            for d in range(zs):
                for e in range(2):
                    sum1(par, p, e, d).wait_send()
                sum2(par, p, d).wait_send()
                if d:
                    sum3(par, p, d).wait_send()

    def fetch(which, k, buf):
        at = pl.ds(pl.multiple_of(k * tile, tile), tile)
        return (
            pltpu.make_async_copy(k_hbm.at[which, :, :, at], kbuf.at[buf], k_sem.at[buf, 0]),
            pltpu.make_async_copy(place_hbm.at[:, at], pbuf.at[buf], k_sem.at[buf, 1]),
        )

    def fetch_start(which, k, buf):
        for copy in fetch(which, k, buf):
            copy.start()

    def fetch_wait(which, k, buf):
        for copy in fetch(which, k, buf):
            copy.wait()

    def slots_step(h, k, buf, sign):
        real = jnp.concatenate([x[h, 0, 2 * k], x[h, 0, 2 * k + 1]], axis=1)
        imag = jnp.concatenate([x[h, 1, 2 * k], x[h, 1, 2 * k + 1]], axis=1)
        high, low = split(jnp.concatenate([real, imag], axis=0))
        high2, low2 = split(jnp.concatenate([imag * (-sign), real * sign], axis=0))
        place = pbuf[buf]
        ug[0] += (
            mm(high, kbuf[buf, 0], NT)
            + mm(low, kbuf[buf, 0], NT)
            + mm(high, kbuf[buf, 1], NT)
            + mm(high2, kbuf[buf, 2], NT)
            + mm(low2, kbuf[buf, 2], NT)
            + mm(high2, kbuf[buf, 3], NT)
        )
        ug[1] += mm(high, place, NT) + mm(low, place, NT)

    def vecs_make(sign):
        def total(t):
            return ug[t] + jnp.concatenate([ug_got[t, :, half:], ug_got[t, :, :half]], axis=1)

        vecs[0], vecs[1] = split(total(0))
        vec = total(1)
        vecs[2], vecs[3] = split(vec)
        vecs[4], vecs[5] = split(
            jnp.concatenate([vec[step_cols:] * (-sign), vec[:step_cols] * sign], axis=0)
        )

    def sources_step(par, k, buf):
        place = pbuf[buf]
        out = (
            mm(vecs[2], kbuf[buf, 0], NN)
            + mm(vecs[3], kbuf[buf, 0], NN)
            + mm(vecs[2], kbuf[buf, 1], NN)
            + mm(vecs[4], kbuf[buf, 2], NN)
            + mm(vecs[5], kbuf[buf, 2], NN)
            + mm(vecs[4], kbuf[buf, 3], NN)
            + mm(vecs[0], place, NN)
            + mm(vecs[1], place, NN)
        )
        for p in range(2):
            for e in range(2):
                v[par, p, 2 * k + e] = out[
                    p * step_cols : (p + 1) * step_cols, e * width : (e + 1) * width
                ]

    def receivers(k):
        q, d = k // zs, k % zs
        col = (j + q) % 2 + 2 * ((j // 2 + q // 2) % 2)
        return col * rows + (z + d) % zs * 2

    def lanes(at):
        return pl.ds(pl.multiple_of(at * width, width), width)

    def swap(k):
        return remote(
            traces_hbm.at[:, :, lanes(receivers(k) + 1 - core)], got_hbm.at[k],
            swap_send.at[k], swap_recv.at[k], other,
        )

    def load(k, buf):
        return (
            pltpu.make_async_copy(
                traces_hbm.at[:, :, lanes(receivers(k) + core)], tbuf.at[buf, 0],
                in_sem.at[buf, 0],
            ),
            pltpu.make_async_copy(got_hbm.at[k], tbuf.at[buf, 1], in_sem.at[buf, 1]),
        )

    def load_start(k, buf):
        swap(k).wait_recv()
        for copy in load(k, buf):
            copy.start()

    def store(k, buf):
        return [
            pltpu.make_async_copy(
                kbuf.at[buf, :, :, pl.ds(which * width, width)],
                k_hbm.at[which, :, :, lanes(k)],
                out_sem.at[buf, which],
            )
            for which in range(2)
        ] + [
            pltpu.make_async_copy(
                pbuf.at[buf, :, pl.ds(0, width)], place_hbm.at[:, lanes(k)], out_sem.at[buf, 2]
            )
        ]

    def prepare_step(k, buf):
        part_slots = tbuf.shape[2]
        at = lanes(k)
        for half_at in range(2):
            these = pl.ds(half_at * part_slots, part_slots)
            hot = hot_ref[these, :]
            own = mm(hot, recorded_ref[:, at], NN) > 0.5
            mir = mm(hot, mirrored_ref[:, at], NN) > 0.5
            pbuf[buf, these, pl.ds(0, width)] = jnp.where(
                ids_ref[these, :] == target_ref[:, at], 1.0, 0.0
            ).astype(jnp.bfloat16)
            for part in range(2):
                high, low = split(tbuf[buf, half_at, :, part, :])
                for n, piece in enumerate((high, low)):
                    wide = piece.astype(jnp.float32)
                    for which, mask in enumerate((own, mir)):
                        kbuf[buf, 2 * part + n, these, pl.ds(which * width, width)] = jnp.where(
                            mask, wide, 0.0
                        ).astype(jnp.bfloat16)

    def loop(low, high, body):
        def step(i, carry):
            body(i)
            return carry

        lax.fori_loop(low, high, step, 0)

    barrier = pltpu.get_barrier_semaphore()
    for peer in peers:
        pl.semaphore_signal(
            barrier, inc=1, device_id=peer, device_id_type=pl.DeviceIdType.MESH
        )

    @pl.when(jnp.logical_not(stays))
    def _():
        for peer in (goal, origin):
            pl.semaphore_signal(
                barrier, inc=1, device_id=peer, device_id_type=pl.DeviceIdType.MESH
            )

    def own_piece(h, p):
        return pltpu.make_async_copy(
            panel_hbm.at[p, h], x.at[h, p, 0], panel_sem.at[h * 2 + p]
        )

    for h in range(pieces):
        for p in range(2):
            own_piece(h, p).start()
    for h in range(pieces):
        for p in range(2):
            own_piece(h, p).wait()

    @pl.when(stays)
    def _():
        pl.semaphore_wait(barrier, len(peers))

    @pl.when(jnp.logical_not(stays))
    def _():
        pl.semaphore_wait(barrier, len(peers) + 2)

    count = cols * zs
    loop(0, 2, spread_line)
    loop(0, count, lambda k: swap(k).start())
    load_start(0, 0)

    def prepare_pair(i):
        for e in range(2):
            k = 2 * i + e
            if e == 0:
                load_start(k + 1, 1)
            else:

                @pl.when(k + 1 < count)
                def _():
                    load_start(k + 1, 0)

            for copy in load(k, e):
                copy.wait()

            @pl.when(i > 0)
            def _():
                for copy in store(k - 2, e):
                    copy.wait()

            prepare_step(k, e)
            for copy in store(k, e):
                copy.start()
        h, d = i // zs, i % zs

        @pl.when(d > 0)
        def _():
            spread_more(h, d)

    loop(0, count // 2, prepare_pair)
    for e in range(2):
        for copy in store(count - 2 + e, e):
            copy.wait()
    loop(0, count, lambda k: swap(k).wait_send())
    fetch_start(0, 0, 0)
    loop(0, zs, lambda d: spread_last(0, d))

    def turn_of(t):
        for n, peer in enumerate(peers):
            pl.semaphore_signal(
                ready.at[n], inc=1, device_id=peer, device_id_type=pl.DeviceIdType.MESH
            )
        for n in range(len(peers)):
            pl.semaphore_wait(ready.at[n], 1)
        h, phase, par = t % pieces, t // pieces, t % 2
        sign = (1 - 2 * phase).astype(jnp.float32)
        computes = t < 2 * pieces
        sums = t > 0
        spreads = t < pieces + 2
        h_sum, phase_sum, par_sum = (t + pieces - 1) % pieces, (t - 1) // pieces, (t + 1) % 2
        h_spread = (t + pieces - 2) % pieces
        lasts, h_last = t < pieces + 3, (t + 1) % pieces

        @pl.when(sums)
        def _():
            sum_first(par_sum)

        @pl.when(spreads)
        def _():
            spread_line(h_spread)

        @pl.when(computes)
        def _():
            spread_end(h)
            ug[...] = jnp.zeros_like(ug)

        def first_half(d):
            @pl.when(computes)
            def _():
                for e in range(2):
                    k = 2 * d + e
                    fetch_wait(phase, k, e)
                    if e == 0:
                        fetch_start(phase, k + 1, 1)
                    else:
                        more = k + 1 < tiles

                        @pl.when(more)
                        def _():
                            fetch_start(phase, k + 1, 0)

                        @pl.when(jnp.logical_not(more))
                        def _():
                            fetch_start(1 - phase, 0, 0)

                    slots_step(h, k, e, sign)

            @pl.when(d < zs - 1)
            def _():
                first_tick(d)

        def first_tick(d):
            @pl.when(sums)
            def _():
                sum_second(par_sum, d)

            @pl.when(lasts)
            def _():
                spread_last(h_last, d)

        loop(0, zs, first_half)
        trade = remote(ug, ug_got, ug_sem.at[0], ug_sem.at[1], other)

        @pl.when(computes)
        def _():
            trade.start()

        first_tick(zs - 1)

        @pl.when(computes)
        def _():
            trade.wait()
            vecs_make(sign)

        def second_half(d):
            @pl.when(computes)
            def _():
                for e in range(2):
                    k = 2 * d + e
                    fetch_wait(1 - phase, k, e)
                    if e == 0:
                        fetch_start(1 - phase, k + 1, 1)
                    else:

                        @pl.when(k + 1 < tiles)
                        def _():
                            fetch_start(1 - phase, k + 1, 0)

                        @pl.when(jnp.logical_and(k + 1 == tiles, t + 1 < 2 * pieces))
                        def _():
                            fetch_start((t + 1) // pieces, 0, 0)

                    sources_step(par, k, e)

            @pl.when(sums)
            def _():
                sum_third(par_sum, d)

            @pl.when(jnp.logical_and(spreads, d > 0))
            def _():
                spread_more(h_spread, d)

        loop(0, zs, second_half)

        @pl.when(sums)
        def _():
            sum_end(par_sum, h_sum, phase_sum)

    loop(0, 2 * pieces + 1, turn_of)
    loop(0, pieces, lambda h: deliver(h, "wait"))


def mega(panel, traces, weights, ids, hot, recorded, mirrored, target, zs, pieces):
    _, focus, width = panel.shape
    part_slots = traces.shape[0]
    slots = 2 * part_slots
    step = focus // pieces
    blocks = 4 * zs
    length = blocks * width
    panel = panel.reshape(2, pieces, step, width)
    vmem = pl.BlockSpec(memory_space=pltpu.VMEM)
    hbm = pl.BlockSpec(memory_space=pl.ANY)
    f32, b16 = jnp.float32, jnp.bfloat16
    dma = pltpu.SemaphoreType.DMA
    shape = jax.ShapeDtypeStruct((pieces, 2, step, width), f32)
    return pl.pallas_call(
        functools.partial(mega_kernel, zs, pieces),
        in_specs=[hbm, hbm] + [vmem] * 6,
        out_specs=[vmem, vmem, hbm, hbm, hbm],
        out_shape=[
            shape,
            shape,
            jax.ShapeDtypeStruct((2, 4, slots, length), b16),
            jax.ShapeDtypeStruct((slots, length), b16),
            jax.ShapeDtypeStruct((blocks, part_slots, 2, width), f32),
        ],
        scratch_shapes=[
            pltpu.VMEM((pieces, 2, blocks, step, width), f32),
            pltpu.VMEM((2, 2, blocks, step, width), f32),
            pltpu.VMEM((2, 2, zs, step, width), f32),
            pltpu.VMEM((2, zs, step, width), f32),
            pltpu.VMEM((2, zs, step, width), f32),
            pltpu.VMEM((2, 2 * step, slots), f32),
            pltpu.VMEM((2, 2 * step, slots), f32),
            pltpu.VMEM((6, 2 * step, slots), b16),
            pltpu.VMEM((2, 4, slots, 2 * width), b16),
            pltpu.VMEM((2, slots, 2 * width), b16),
            pltpu.VMEM((2, 2, part_slots, 2, width), f32),
            pltpu.VMEM((pieces, 2, step, width), f32),
            dma((pieces, 8 * zs)),
            dma((pieces, 8 * zs)),
            dma((8 * zs,)),
            dma((8 * zs,)),
            dma((2,)),
            dma((2, 2)),
            pltpu.SemaphoreType.REGULAR((zs + 2,)),
            dma((2 * pieces,)),
            dma((blocks,)),
            dma((blocks,)),
            dma((2, 2)),
            dma((2, 3)),
            dma((pieces,)),
            dma((pieces,)),
        ],
        compiler_params=pltpu.CompilerParams(
            collective_id=0, has_side_effects=True, vmem_limit_bytes=MEGA_VMEM
        ),
        name="products",
    )(panel, traces, weights, ids, hot, recorded, mirrored, target)[:2]


def lookup(bins, table):
    matches = bins[:, None] == jnp.arange(table.shape[0], dtype=jnp.int32)[None, :]
    return jnp.sum(jnp.where(matches, table[None, :], 0.0), axis=1)


def local(
    zs, cols, shot_traces, shot_ids, shot_counts, missing_blocks, weight_bins, weight_table,
    focus_panel
):
    slots, _, stations = shot_traces.shape
    focus = focus_panel.shape[2]
    width = focus_panel.shape[1]
    rows = 2 * zs
    z, core, j = (lax.axis_index(name) for name in AXES)
    bits = [1 << b for b in range(cols.bit_length() - 1)]
    assert 1 << len(bits) == cols

    def device(a, c, b):
        return (a * 2 + c) * cols + b

    everyone = [(a, c, b) for a in range(zs) for c in range(2) for b in range(cols)]

    def send(x, target):
        return lax.ppermute(x, AXES, [(device(*d), device(*target(*d))) for d in everyone])

    def across_core(x):
        return send(x, lambda a, c, b: (a, 1 - c, b))

    def gather(piece, order):
        group = [piece] + [
            send(piece, lambda a, c, b, d=d: ((a - d) % zs, c, b)) for d in range(1, zs)
        ]
        size = zs * width
        groups = {0: jnp.concatenate(group, axis=1)}
        for bit in order:
            keys = sorted(groups)
            got = send(
                jnp.concatenate([groups[k] for k in keys], axis=1),
                lambda a, c, b: (a, c, b ^ bit),
            )
            for n, k in enumerate(keys):
                groups[k | bit] = got[:, n * size : (n + 1) * size]
        return jnp.concatenate([groups[k] for k in range(cols)], axis=1)

    def scatter(total, order):
        size = zs * width
        groups = {k: total[:, k * size : (k + 1) * size] for k in range(cols)}
        for bit in order:
            away = sorted(k for k in groups if k & bit)
            got = send(
                jnp.concatenate([groups[k] for k in away], axis=1),
                lambda a, c, b: (a, c, b ^ bit),
            )
            for n, k in enumerate(away):
                groups[k ^ bit] = groups[k ^ bit] + got[:, n * size : (n + 1) * size]
                del groups[k]
        line = groups[0]
        out = line[:, :width]
        for d in range(1, zs):
            out = out + send(
                line[:, d * width : (d + 1) * width],
                lambda a, c, b: ((a + d) % zs, c, b),
            )
        return out

    order_re, order_im = bits, bits[::-1]

    rel = [(q, d) for q in range(cols) for d in range(zs)]
    places = jnp.stack(
        [lax.bitwise_xor(j, jnp.int32(q)) * rows + lax.rem(z + d, zs) * 2 for q, d in rel]
    ).astype(jnp.int32)
    keep_at, away_at = places + core, places + 1 - core
    counted = jnp.where(jnp.arange(slots, dtype=jnp.int32) < shot_counts[0], shot_ids, -1)
    ids = jnp.concatenate([counted, across_core(counted)])[:, None]
    down, over = missing_blocks.shape
    missing = lax.dynamic_update_slice(
        jnp.zeros((rows * down, cols * over), jnp.int32),
        missing_blocks,
        ((z * 2 + core) * down, j * over),
    )
    assert zs & (zs - 1) == 0
    missing = missing + across_core(missing)
    for bit in bits:
        missing = missing + send(missing, lambda a, c, b: (a, c, b ^ bit))
    for bit in (1 << n for n in range(zs.bit_length() - 1)):
        missing = missing + send(missing, lambda a, c, b: (a ^ bit, c, b))
    missing = missing.astype(jnp.bfloat16)
    blocks = missing.shape[0]
    side = stations // blocks
    hot = jnp.where(ids // side == jnp.arange(blocks, dtype=jnp.int32)[None, :], 1.0, 0.0)
    hot = jnp.where(ids >= 0, hot, 0.0).astype(jnp.bfloat16)
    target = (keep_at[:, None] * width + jnp.arange(width, dtype=jnp.int32)[None, :]).reshape(1, -1)
    spread = jnp.where(
        target // side == jnp.arange(blocks, dtype=jnp.int32)[:, None], 1.0, 0.0
    ).astype(jnp.bfloat16)
    recorded = mm(1 - missing, spread, NN).astype(jnp.bfloat16)
    mirrored = mm(missing.T, spread, NN).astype(jnp.bfloat16)

    pairs = []
    for n in range(rows * cols):
        i, b = n % rows, n // rows
        pairs.append((n, i * cols + b))
    bins = lax.ppermute(weight_bins, AXES, pairs)
    weights = lookup(bins, weight_table)[None, :]
    back = [(b, a) for a, b in pairs]

    def product(real, imag, first, second, sign):
        real, imag = gather(real, order_re), gather(imag, order_im)
        mine = to_slots(real, imag, first, place, sign)
        real, imag = from_slots(mine, across_core(mine), second, place, sign)
        return scatter(real, order_re), scatter(imag, order_im)

    panel = focus_panel.transpose(0, 2, 1)
    if cols == 4 and width % 128 == 0:
        outs = mega(
            panel, shot_traces, weights, ids, hot, recorded, mirrored, target, zs, TURNS
        )
        return tuple(out.transpose(1, 3, 0, 2).reshape(2, width, focus) for out in outs)
    step = focus // PIECES
    away, keep = pack(shot_traces, away_at, keep_at, width)
    got = across_core(away)
    kernels, place = prepare(keep, got, ids, hot, recorded, mirrored, target)
    own, mir = kernels[0], kernels[1]
    fields, images = [], []
    for h in range(PIECES):
        at = slice(h * step, (h + 1) * step)
        real, imag = product(panel[0, at], panel[1, at], own, mir, 1)
        fields.append(jnp.stack([real, imag]))
        real, imag = product(real * weights, imag * weights, mir, own, -1)
        images.append(jnp.stack([real, imag]))
    field = lax.ppermute(jnp.concatenate(fields, axis=1), AXES, back)
    return field.transpose(0, 2, 1), jnp.concatenate(images, axis=1).transpose(0, 2, 1)


def solution(mesh):
    rows, cols = mesh.shape["row"], mesh.shape["col"]
    zs = rows // 2
    split_mesh = Mesh(mesh.devices.reshape(zs, 2, cols), AXES)
    rowwise = ("z", "core", "col")
    colwise = ("col", "z", "core")
    placed = (
        P(rowwise, None, None),
        P(rowwise),
        P(rowwise),
        P(("z", "core"), "col"),
        P(rowwise),
        P(),
        P(None, colwise, None),
    )
    return jax.shard_map(
        functools.partial(local, zs, cols),
        mesh=split_mesh,
        in_specs=placed,
        out_specs=(P(None, rowwise, None), P(None, colwise, None)),
        check_vma=False,
    )
```
